768 devices in a mesh: lat: 16 (over z_lo, x), lon: 6 (over z_hi, core), opt: 8 (over y).
Axes of the slice: x: 4, y: 8, z: 12 (z_hi: 3, z_lo: 4; z = z_hi * 4 + z_lo), core: 2. Of those that a mesh axis runs over, the one named last changes fastest.
Arguments:
- queries: bfloat16 [8, 16, 6, 128, 512], P('opt', 'lat', 'lon'), may hold values from -8 to 8
- keys: bfloat16 [8, 16, 6, 128, 512], P('opt', 'lat', 'lon'), may hold values from -8 to 8
- values: bfloat16 [8, 16, 6, 128, 512], P('opt', 'lat', 'lon'), may hold values from -6 to 6
- grad_out: bfloat16 [8, 16, 6, 128, 1024], P('opt', 'lat', 'lon'), may hold values from -6 to 6
- w_out: bfloat16 [512, 1024], replicated, may hold values from -0.25 to 0.25
- pattern: int32 [16, 6, 9], replicated, may hold values from 0 to 1, as said below
Outputs:
- grad_queries: bfloat16 [8, 16, 6, 128, 512], P('opt', 'lat', 'lon')
- grad_keys: bfloat16 [8, 16, 6, 128, 512], P('opt', 'lat', 'lon')
- grad_values: bfloat16 [8, 16, 6, 128, 512], P('opt', 'lat', 'lon')
- grad_w_out: float32 [512, 1024], P('opt')
The draws below stay inside these ranges and needn't reach their ends.
Inputs may be any that keep to these rules, and one draw needn't show every extreme that they name: `pattern`: entry 4 of each block's nine (the block itself) is 1.
All inputs are finite; a program needn't handle non-finite values.
Results may differ from the reference program's by a relative error of at most 0.034.
Values may be sent and summed in bfloat16 or wider, within the bound.
No kernel may reach another device: no remote copies, remote signals or barrier semaphores. Data moves between devices by JAX's collectives and lax.ppermute only.
A program may use at most 32 MiB of HBM per device.

```python
import jax
import jax.numpy as jnp
from jax import lax

D = 1024
HEADS = 8
HDIM = 64
BLOCK = 128
DA = 512
NBL = 16
NBO = 6
SAMPLES = 8


def paired_draw(key, role):
    shape = (SAMPLES, NBL, NBO, BLOCK, HEADS * HDIM)
    result = jnp.clip(1.4 * jax.random.normal(jax.random.fold_in(key, 11 + role), shape, jnp.float32), -8.0, 8.0)
    return result.astype(jnp.bfloat16)


def draw_queries(key, part):
    return paired_draw(key, 0)


def draw_keys(key, part):
    return paired_draw(key, 1)


def draw_pattern(key, part):
    shape = (NBL, NBO, 9)
    coins = jax.random.randint(jax.random.fold_in(key, 7), shape, 0, 2)
    centre = lax.broadcasted_iota(jnp.int32, shape, 2) == 4
    return jnp.where(centre, 1, coins).astype(jnp.int32)


def shard_levels(stream_key, shape, shards, smallest, largest):
    factor_of, own = 1.0, jax.random.fold_in(stream_key, 6)
    for axis_at, blocks in shards:
        heights = jnp.exp(jax.random.uniform(jax.random.fold_in(own, axis_at), (blocks,), jnp.float32, smallest / len(shards), largest / len(shards)))
        factor_of = factor_of * jnp.repeat(heights, shape[axis_at] // blocks).reshape([-1 if axis == axis_at else 1 for axis in range(len(shape))])
    return factor_of


def bell_draw(rng, shape, deviation, most, cuts=(), held_as=jnp.bfloat16):
    values = jax.random.normal(rng, shape, jnp.float32) * deviation
    if len(cuts) > 0:
        values = shard_levels(rng, shape, cuts, -0.22, 0.18) * values
    return jnp.clip(values, min=-most, max=most).astype(held_as)


def setup_inputs(seed: int = 0) -> dict:
    splits = jax.random.split(jax.random.key(seed), 7)
    return {
        "queries": draw_queries(jax.random.fold_in(splits[6], 71), 0),
        "keys": draw_keys(jax.random.fold_in(splits[6], 71), 0),
        "values": bell_draw(splits[2], (SAMPLES, NBL, NBO, BLOCK, DA), 1.0, 6.0, ((0, 8), (1, 16), (2, 6))),
        "grad_out": bell_draw(splits[3], (SAMPLES, NBL, NBO, BLOCK, D), 1.0, 6.0, ((0, 8), (1, 16), (2, 6))),
        "w_out": bell_draw(splits[4], (DA, D), DA ** -0.5, 0.25),
        "pattern": draw_pattern(jax.random.fold_in(splits[6], 71), 0),
    }


def rounded(values_in):
    return lax.optimization_barrier(values_in.astype(jnp.bfloat16)).astype(jnp.float32)


def shifted(field, lat_step, lon_step):
    moved = jnp.roll(field, -lon_step, axis=1)
    if lat_step == 1:
        moved = jnp.concatenate([moved[1:], jnp.zeros_like(moved[:1])], axis=0)
    elif lat_step == -1:
        moved = jnp.concatenate([jnp.zeros_like(moved[:1]), moved[:-1]], axis=0)
    return moved


def lat_ok(lat_step):
    rows = jnp.arange(NBL, dtype=jnp.int32) + lat_step
    return ((rows >= 0) & (rows < NBL))[:, None]


def one_sample(query_in, key_in, value_in, grad_in, w_out, pattern):
    score_scale = HDIM ** -0.5
    head_shape = (NBL, NBO, BLOCK, HEADS, HDIM)
    query_heads = query_in.astype(jnp.float32).reshape(head_shape)
    key_heads = key_in.astype(jnp.float32).reshape(head_shape)
    value_heads = value_in.astype(jnp.float32).reshape(head_shape)
    directions = [(lat_step, lon_step) for lat_step in (-1, 0, 1) for lon_step in (-1, 0, 1)]

    def scores_of(index):
        lat_step, lon_step = directions[index]
        near_keys = shifted(key_heads, lat_step, lon_step)
        scores = jnp.einsum("abqhe,abkhe->abhqk", query_heads, near_keys) * score_scale
        live = (pattern[:, :, index] > 0) & lat_ok(lat_step)
        return scores, live[:, :, None, None, None], near_keys

    row_max = jnp.full((NBL, NBO, HEADS, BLOCK), -jnp.inf, dtype=jnp.float32)
    for index in range(9):
        scores, live, unused = scores_of(index)
        row_max = jnp.maximum(row_max, jnp.max(jnp.where(live, scores, -jnp.inf), axis=-1))
    total = jnp.zeros((NBL, NBO, HEADS, BLOCK), jnp.float32)
    for index in range(9):
        scores, live, unused = scores_of(index)
        total = total + jnp.sum(jnp.where(live, jnp.exp(scores - row_max[..., None]), 0.0), axis=-1)
    log_norm = row_max + jnp.log(total)
    attended = jnp.zeros(head_shape, jnp.float32)
    for index in range(9):
        lat_step, lon_step = directions[index]
        scores, live, unused = scores_of(index)
        softmax_w = jnp.where(live, jnp.exp(scores - log_norm[..., None]), 0.0)
        near_values = shifted(value_heads, lat_step, lon_step)
        attended = attended + jnp.einsum("abhqk,abkhe->abqhe", rounded(softmax_w), near_values)
    attended_low = attended.astype(jnp.bfloat16)
    grad_att = jnp.dot(grad_in.reshape(-1, D), w_out.T, preferred_element_type=jnp.float32).astype(jnp.bfloat16)
    grad_heads = grad_att.astype(jnp.float32).reshape(head_shape)
    row_delta = jnp.transpose(jnp.sum(grad_heads * attended_low.astype(jnp.float32), axis=-1), (0, 1, 3, 2))
    grad_query = jnp.zeros(head_shape, jnp.float32)
    grad_key = jnp.zeros(head_shape, jnp.float32)
    grad_value = jnp.zeros(head_shape, jnp.float32)
    for index in range(9):
        lat_step, lon_step = directions[index]
        scores, live, near_keys = scores_of(index)
        near_values = shifted(value_heads, lat_step, lon_step)
        softmax_w = jnp.where(live, jnp.exp(scores - log_norm[..., None]), 0.0)
        softmax_low = rounded(softmax_w)
        grad_prob = jnp.einsum("abqhe,abkhe->abhqk", grad_heads, near_values)
        grad_score = rounded(softmax_w * (grad_prob - row_delta[..., None]))
        grad_query = grad_query + jnp.einsum("abhqk,abkhe->abqhe", grad_score, near_keys) * score_scale
        key_part = jnp.einsum("abhqk,abqhe->abkhe", grad_score, query_heads) * score_scale
        value_part = jnp.einsum("abhqk,abqhe->abkhe", softmax_low, grad_heads)
        grad_key = grad_key + shifted(key_part, -lat_step, -lon_step)
        grad_value = grad_value + shifted(value_part, -lat_step, -lon_step)
    flat_shape = (NBL, NBO, BLOCK, DA)
    return (grad_query.reshape(flat_shape).astype(jnp.bfloat16), grad_key.reshape(flat_shape).astype(jnp.bfloat16),
            grad_value.reshape(flat_shape).astype(jnp.bfloat16), attended_low.reshape(flat_shape))


def reference(queries, keys, values, grad_out, w_out, pattern):
    def per_sample(inputs):
        return one_sample(inputs[0], inputs[1], inputs[2], inputs[3], w_out, pattern)

    grad_queries, grad_keys, grad_values, attended = lax.map(per_sample, (queries, keys, values, grad_out))
    grad_w_out = jnp.dot(attended.reshape(-1, DA).T, grad_out.reshape(-1, D), preferred_element_type=jnp.float32)
    return (grad_queries, grad_keys, grad_values, grad_w_out)
```

```python
import jax
import jax.numpy as jnp
from jax import lax
from jax.sharding import PartitionSpec as P

HDIM = 64
SCALE = HDIM ** (-0.5)


def around(array, axis, by):
    count = lax.axis_size(axis)
    return lax.ppermute(array, axis, [(i, (i + by) % count) for i in range(count)])


def along(array, axis, by):
    count = lax.axis_size(axis)
    return lax.ppermute(array, axis, [(i, i + by) for i in range(count) if 0 <= i + by < count])


def to_all(array, axis):
    count = lax.axis_size(axis)
    return lax.all_to_all(jnp.broadcast_to(array[None], (count,) + array.shape), axis, 0, 0)


def heads_of(array):
    return array.reshape(array.shape[:-1] + (array.shape[-1] // HDIM, HDIM))


def attention(query, dout, near_keys, near_values, live):
    query_heads, dout_heads = heads_of(query), heads_of(dout)
    keys, values = heads_of(near_keys), heads_of(near_values)
    live = live[None, None, :, None]
    scores = (
        jnp.einsum("qhe,dkhe->hqdk", query_heads, keys, preferred_element_type=jnp.float32)
        * SCALE
    )
    row_max = jnp.max(jnp.where(live, scores, -jnp.inf), axis=(2, 3))
    weights = jnp.where(live, jnp.exp(scores - row_max[:, :, None, None]), 0.0)
    log_norm = row_max + jnp.log(jnp.sum(weights, axis=(2, 3)))
    prob = jnp.where(live, jnp.exp(scores - log_norm[:, :, None, None]), 0.0)
    prob_low = prob.astype(jnp.bfloat16)
    attended = jnp.einsum(
        "hqdk,dkhe->qhe", prob_low, values, preferred_element_type=jnp.float32
    ).astype(jnp.bfloat16)
    row_delta = jnp.sum(dout_heads.astype(jnp.float32) * attended.astype(jnp.float32), axis=2).T
    grad_prob = jnp.einsum("qhe,dkhe->hqdk", dout_heads, values, preferred_element_type=jnp.float32)
    grad_score = (prob * (grad_prob - row_delta[:, :, None, None])).astype(jnp.bfloat16)
    grad_query = (
        jnp.einsum("hqdk,dkhe->qhe", grad_score, keys, preferred_element_type=jnp.float32) * SCALE
    )
    key_part = (
        jnp.einsum("hqdk,qhe->dkhe", grad_score, query_heads, preferred_element_type=jnp.float32)
        * SCALE
    )
    value_part = jnp.einsum(
        "hqdk,qhe->dkhe", prob_low, dout_heads, preferred_element_type=jnp.float32
    )
    flat = query.shape
    pair = jnp.stack((key_part, value_part), axis=1).reshape((9, 2) + flat)
    return attended.reshape(flat), grad_query.astype(jnp.bfloat16).reshape(flat), pair


def shards(queries, keys, values, grad_out, w_out, pattern):
    low, wide = jnp.bfloat16, jnp.float32
    query, key, value, grad = queries[0, 0, 0], keys[0, 0, 0], values[0, 0, 0], grad_out[0, 0, 0]
    block_len, att_width = query.shape
    model_width = grad.shape[1]
    lat_count, opt_count = lax.axis_size("lat"), lax.axis_size("opt")
    at_lat, at_lon = lax.axis_index("lat"), lax.axis_index("lon")

    own = jnp.stack((key, value))
    left, right = around(own, "lon", 1), around(own, "lon", -1)
    row = jnp.stack((left, own, right))
    above, below = along(row, "lat", 1), along(row, "lat", -1)
    grads_of_samples = to_all(grad, "opt")

    dout = lax.dot_general(
        grad, w_out, (((1,), (1,)), ((), ())), preferred_element_type=wide
    ).astype(low)
    flags = lax.dynamic_slice(pattern, (at_lat, at_lon, 0), (1, 1, 9)).reshape(9)
    key_rows = at_lat + jnp.arange(9) // 3 - 1
    live = (flags > 0) & (key_rows >= 0) & (key_rows < lat_count)

    near = jnp.stack((above, row, below)).reshape(9, 2, block_len, att_width)
    near, grads_of_samples = lax.optimization_barrier((near, grads_of_samples))
    attended, grad_query, pair = attention(query, dout, near[:, 0], near[:, 1], live)

    attended_of_samples = lax.all_to_all(
        attended.T.reshape(opt_count, att_width // opt_count, block_len), "opt", 0, 0
    )
    w_part = jnp.einsum(
        "srt,stc->rc", attended_of_samples, grads_of_samples, preferred_element_type=wide
    ).astype(low)
    w_rows = w_part.shape[0] // lat_count
    w_part = lax.all_to_all(w_part.reshape(lat_count, w_rows, model_width), "lat", 0, 0)
    w_part = jnp.sum(w_part.astype(wide), axis=0).astype(low)
    w_part = jnp.sum(to_all(w_part, "lon").astype(wide), axis=0).astype(low)
    grad_weight = to_all(w_part, "lat").reshape(lat_count * w_rows, model_width).astype(wide)

    pair = pair.reshape(3, 3, 2, block_len, att_width)
    up, down = along(pair[0].astype(low), "lat", -1), along(pair[2].astype(low), "lat", 1)
    sums = pair[1] + up.astype(wide) + down.astype(wide)
    from_right, from_left = around(sums[0].astype(low), "lon", -1), around(sums[2].astype(low), "lon", 1)
    owned = (sums[1] + from_right.astype(wide) + from_left.astype(wide)).astype(low)
    return (
        grad_query[None, None, None],
        owned[0][None, None, None],
        owned[1][None, None, None],
        grad_weight,
    )


def solution(mesh):
    blocks = P("opt", "lat", "lon", None, None)
    return jax.shard_map(
        shards,
        mesh=mesh,
        in_specs=(blocks, blocks, blocks, blocks, P(), P()),
        out_specs=(blocks, blocks, blocks, P("opt", None)),
        check_vma=False,
    )
```

```python
import jax
import jax.numpy as jnp
from jax import lax
from jax.experimental import pallas as pl
from jax.experimental.pallas import tpu as pltpu
from jax.sharding import PartitionSpec as P

HDIM = 64
SCALE = HDIM ** (-0.5)
DEAD = -1e30
LANES = 2 * HDIM


def exchange(array, axis, mate):
    pairs = [(i, mate(i)) for i in range(lax.axis_size(axis))]
    return lax.ppermute(array, axis, [(i, j) for i, j in pairs if 0 <= j < lax.axis_size(axis)])


def next_door(i):
    return i ^ 1


def other_door(i):
    return i - 1 if i % 2 == 0 else i + 1


def partner_of(array):
    return exchange(array, "lon", next_door)


def far_of(array):
    count = lax.axis_size("lon")
    return exchange(array, "lon", lambda i: other_door(i) % count)


def lat_mates_of(array):
    return exchange(array, "lat", next_door), exchange(array, "lat", other_door)


def to_all(array, axis):
    count = lax.axis_size(axis)
    return lax.all_to_all(jnp.broadcast_to(array[None], (count,) + array.shape), axis, 0, 0)


def sum_over_lon(part):
    count = lax.axis_size("lon")
    chips = count // 2
    part = part + partner_of(part)
    at = lax.axis_index("lon") // 2
    terms = [part] + [
        lax.ppermute(part, "lon", [(i, (i + 2 * by) % count) for i in range(count)])
        for by in range(1, chips)
    ]
    total = None
    for chip in range(chips):
        term = terms[0]
        for by in range(1, chips):
            term = jnp.where((at - by) % chips == chip, terms[by], term)
        total = term if total is None else total + term
    return total


def attention_kernel(
    live,
    query,
    dout,
    key,
    value,
    partner,
    far,
    pair_p,
    far_p,
    pair_q,
    far_q,
    attended_t,
    grad_query,
    up,
    middle,
    down,
    prob,
):
    wide, low = jnp.float32, jnp.bfloat16
    block_len = query.shape[0]
    first_head = lax.broadcasted_iota(jnp.int32, query.shape, 1) < HDIM

    def apart(array):
        zero = jnp.zeros_like(array)
        return jnp.concatenate(
            [jnp.where(first_head, array, zero), jnp.where(first_head, zero, array)], axis=0
        )

    def joined(array):
        return jnp.concatenate([array[:HDIM, :block_len], array[HDIM:, block_len:]], axis=0)

    def nine(own, at):
        return jnp.concatenate(
            [
                pair_p[0, at], pair_p[1, at], far_p[at],
                partner[at], own[...], far[at],
                pair_q[0, at], pair_q[1, at], far_q[at],
            ],
            axis=0,
        )

    def block(array, at):
        return array[at * block_len : (at + 1) * block_len]

    def dot(left, right, dims):
        return lax.dot_general(left, right, (dims, ((), ())), preferred_element_type=wide)

    query_cat = apart(query[...] * jnp.asarray(SCALE, low))
    dout_cat = apart(dout[...])
    keys, values = nine(key, 0), nine(value, 1)

    scores = dot(keys, query_cat, ((1,), (1,)))
    row_max = None
    for at in range(9):
        part = block(scores, at) + jnp.where(live[at] > 0, 0.0, DEAD)
        prob[at * block_len : (at + 1) * block_len, :] = part
        row_max = part if row_max is None else jnp.maximum(row_max, part)
    row_max = jnp.max(row_max, axis=0, keepdims=True)
    total = None
    for at in range(9):
        part = jnp.exp(prob[at * block_len : (at + 1) * block_len, :] - row_max)
        prob[at * block_len : (at + 1) * block_len, :] = part
        total = part if total is None else total + part
    norm = 1.0 / jnp.sum(total, axis=0, keepdims=True)
    low_parts = []
    for at in range(9):
        part = prob[at * block_len : (at + 1) * block_len, :] * norm
        prob[at * block_len : (at + 1) * block_len, :] = part
        low_parts.append(part.astype(low))
    prob_low = jnp.concatenate(low_parts, axis=0)
    attended = joined(dot(values.T, prob_low, ((1,), (0,)))).astype(low)
    attended_t[...] = attended

    product = dout[...].T.astype(wide) * attended.astype(wide)
    row_delta = jnp.concatenate(
        [
            jnp.sum(product[:HDIM], axis=0, keepdims=True),
            jnp.sum(product[HDIM:], axis=0, keepdims=True),
        ],
        axis=1,
    )
    grad_prob = dot(values, dout_cat, ((1,), (1,)))
    grad_score = jnp.concatenate(
        [
            (
                prob[at * block_len : (at + 1) * block_len, :] * (block(grad_prob, at) - row_delta)
            ).astype(low)
            for at in range(9)
        ],
        axis=0,
    )
    grad_query[...] = (joined(dot(keys.T, grad_score, ((1,), (0,)))) * SCALE).T.astype(low)
    grad_keys = dot(grad_score, query_cat, ((1,), (0,)))
    grad_values = dot(prob_low, dout_cat, ((1,), (0,)))
    for row, out in enumerate((up, middle, down)):
        for column in range(3):
            out[column, 0] = block(grad_keys, row * 3 + column).astype(out.dtype)
            out[column, 1] = block(grad_values, row * 3 + column).astype(out.dtype)


def attention(live, query, dout, near):
    block_len, width = query.shape
    low, wide = query.dtype, jnp.float32
    one = pl.BlockSpec((block_len, LANES), lambda p: (0, p))
    two = pl.BlockSpec((2, block_len, LANES), lambda p: (0, 0, p))
    four = pl.BlockSpec((2, 2, block_len, LANES), lambda p: (0, 0, 0, p))
    pairs = pl.BlockSpec((3, 2, block_len, LANES), lambda p: (0, 0, 0, p))
    shape = jax.ShapeDtypeStruct
    return pl.pallas_call(
        attention_kernel,
        grid=(width // LANES,),
        in_specs=[pl.BlockSpec(memory_space=pltpu.SMEM), one, one, one, one, two, two, four, two, four, two],
        out_specs=[pl.BlockSpec((LANES, block_len), lambda p: (p, 0)), one, pairs, pairs, pairs],
        out_shape=[
            shape((width, block_len), low),
            shape((block_len, width), low),
            shape((3, 2, block_len, width), low),
            shape((3, 2, block_len, width), wide),
            shape((3, 2, block_len, width), low),
        ],
        scratch_shapes=[pltpu.VMEM((9 * block_len, 2 * block_len), wide)],
        compiler_params=pltpu.CompilerParams(
            dimension_semantics=("arbitrary",), vmem_limit_bytes=40 << 20
        ),
        cost_estimate=pl.CostEstimate(
            flops=12 * 9 * block_len * block_len * width * 2,
            bytes_accessed=8 << 20,
            transcendentals=9 * block_len * block_len * (width // HDIM),
        ),
    )(live, query, dout, *near)


def shards(queries, keys, values, grad_out, w_out, pattern):
    low, wide = jnp.bfloat16, jnp.float32
    query, key, value, grad = queries[0, 0, 0], keys[0, 0, 0], values[0, 0, 0], grad_out[0, 0, 0]
    block_len, att_width = query.shape
    model_width = grad.shape[1]
    lat_count, opt_count = lax.axis_size("lat"), lax.axis_size("opt")
    at_lat, at_lon = lax.axis_index("lat"), lax.axis_index("lon")

    dout = lax.dot_general(
        grad, w_out, (((1,), (1,)), ((), ())), preferred_element_type=wide
    ).astype(low)
    flags = lax.dynamic_slice(pattern, (at_lat, at_lon, 0), (1, 1, 9)).reshape(9)
    at = jnp.arange(9)
    lat_step = (1 - 2 * (at_lat % 2)) * (1 - at // 3)
    lon_step = (1 - 2 * (at_lon % 2)) * (1 - at % 3)
    direction = (lat_step + 1) * 3 + lon_step + 1
    flags = jnp.sum(jnp.where(direction[:, None] == at[None, :], flags[None, :], 0), axis=1)
    key_rows = at_lat + lat_step
    live = ((flags > 0) & (key_rows >= 0) & (key_rows < lat_count)).astype(jnp.int32)

    own = jnp.stack((key, value))
    far, partner = far_of(own), partner_of(own)
    pair_p, pair_q = lat_mates_of(jnp.stack((partner, own)))
    far_p, far_q = lat_mates_of(far)
    grads_of_samples = to_all(grad, "opt")
    attended_t, grad_query, to_p, middle, to_q = attention(
        live, query, dout, (key, value, partner, far, pair_p, far_p, pair_q, far_q)
    )
    attended_t, grads_of_samples = lax.optimization_barrier((attended_t, grads_of_samples))

    attended_of_samples = lax.all_to_all(
        attended_t.reshape(opt_count, att_width // opt_count, block_len), "opt", 0, 0
    )
    w_part = jnp.einsum(
        "srt,stc->rc", attended_of_samples, grads_of_samples, preferred_element_type=wide
    ).astype(low)
    from_p, from_q = exchange(to_p, "lat", next_door), exchange(to_q, "lat", other_door)
    from_p, from_q, w_part = lax.optimization_barrier((from_p, from_q, w_part))
    sums = middle + from_p.astype(wide) + from_q.astype(wide)
    from_far = far_of(sums[2].astype(low))
    from_partner = partner_of(sums[0].astype(low))

    w_rows = w_part.shape[0] // lat_count
    w_part = lax.all_to_all(w_part.reshape(lat_count, w_rows, model_width), "lat", 0, 0)
    w_part = sum_over_lon(jnp.sum(w_part.astype(wide), axis=0)).astype(low)
    grad_weight = to_all(w_part, "lat").reshape(lat_count * w_rows, model_width).astype(wide)

    owned = (sums[1] + from_partner.astype(wide) + from_far.astype(wide)).astype(low)
    return (
        grad_query[None, None, None],
        owned[0][None, None, None],
        owned[1][None, None, None],
        grad_weight,
    )


def solution(mesh):
    blocks = P("opt", "lat", "lon", None, None)
    return jax.shard_map(
        shards,
        mesh=mesh,
        in_specs=(blocks, blocks, blocks, blocks, P(), P()),
        out_specs=(blocks, blocks, blocks, P("opt", None)),
        check_vma=False,
    )
```

```python
import jax
import jax.numpy as jnp
from jax import lax
from jax.experimental import pallas as pl
from jax.experimental.pallas import tpu as pltpu
from jax.sharding import PartitionSpec as P

HDIM = 64
SCALE = HDIM ** (-0.5)
DEAD = -1e30
LANES = 2 * HDIM
PART_ROWS = 8


def exchange(array, axis, mate):
    pairs = [(i, mate(i)) for i in range(lax.axis_size(axis))]
    return lax.ppermute(array, axis, [(i, j) for i, j in pairs if 0 <= j < lax.axis_size(axis)])


def next_door(i):
    return i ^ 1


def other_door(i):
    return i - 1 if i % 2 == 0 else i + 1


def partner_of(array):
    return exchange(array, "lon", next_door)


def far_of(array):
    count = lax.axis_size("lon")
    return exchange(array, "lon", lambda i: other_door(i) % count)


def lat_mates_of(array):
    return exchange(array, "lat", next_door), exchange(array, "lat", other_door)


def to_all(array, axis):
    count = lax.axis_size(axis)
    return lax.all_to_all(jnp.broadcast_to(array[None], (count,) + array.shape), axis, 0, 0)


def attention_kernel(
    live,
    query,
    dout,
    grad,
    key,
    value,
    partner,
    far,
    pair_p,
    far_p,
    pair_q,
    far_q,
    w_parts,
    grad_query,
    up,
    middle,
    down,
    prob,
):
    wide, low = jnp.float32, jnp.bfloat16
    block_len = query.shape[0]
    first_head = lax.broadcasted_iota(jnp.int32, query.shape, 1) < HDIM

    def apart(array):
        zero = jnp.zeros_like(array)
        return jnp.concatenate(
            [jnp.where(first_head, array, zero), jnp.where(first_head, zero, array)], axis=0
        )

    def joined(array):
        return jnp.concatenate([array[:HDIM, :block_len], array[HDIM:, block_len:]], axis=0)

    def nine(own, at):
        return jnp.concatenate(
            [
                pair_p[0, at], pair_p[1, at], far_p[at],
                partner[at], own[...], far[at],
                pair_q[0, at], pair_q[1, at], far_q[at],
            ],
            axis=0,
        )

    def block(array, at):
        return array[at * block_len : (at + 1) * block_len]

    def dot(left, right, dims):
        return lax.dot_general(left, right, (dims, ((), ())), preferred_element_type=wide)

    query_cat = apart(query[...] * jnp.asarray(SCALE, low))
    dout_cat = apart(dout[...])
    keys, values = nine(key, 0), nine(value, 1)

    scores = dot(keys, query_cat, ((1,), (1,)))
    row_max = None
    for at in range(9):
        part = block(scores, at) + jnp.where(live[at] > 0, 0.0, DEAD)
        prob[at * block_len : (at + 1) * block_len, :] = part
        row_max = part if row_max is None else jnp.maximum(row_max, part)
    row_max = jnp.max(row_max, axis=0, keepdims=True)
    total = None
    for at in range(9):
        part = jnp.exp(prob[at * block_len : (at + 1) * block_len, :] - row_max)
        prob[at * block_len : (at + 1) * block_len, :] = part
        total = part if total is None else total + part
    norm = 1.0 / jnp.sum(total, axis=0, keepdims=True)
    low_parts = []
    for at in range(9):
        part = prob[at * block_len : (at + 1) * block_len, :] * norm
        prob[at * block_len : (at + 1) * block_len, :] = part
        low_parts.append(part.astype(low))
    prob_low = jnp.concatenate(low_parts, axis=0)
    attended = joined(dot(values.T, prob_low, ((1,), (0,)))).astype(low)
    w_rows = dot(attended, grad[...], ((1,), (0,)))
    width = w_parts.shape[2]
    across = w_rows.shape[1] // width
    for at in range(w_parts.shape[0]):
        row, column = at // across * PART_ROWS, at % across * width
        w_parts[at] = w_rows[row : row + PART_ROWS, column : column + width].astype(low)

    product = dout[...].T.astype(wide) * attended.astype(wide)
    row_delta = jnp.concatenate(
        [
            jnp.sum(product[:HDIM], axis=0, keepdims=True),
            jnp.sum(product[HDIM:], axis=0, keepdims=True),
        ],
        axis=1,
    )
    grad_prob = dot(values, dout_cat, ((1,), (1,)))
    grad_score = jnp.concatenate(
        [
            (
                prob[at * block_len : (at + 1) * block_len, :] * (block(grad_prob, at) - row_delta)
            ).astype(low)
            for at in range(9)
        ],
        axis=0,
    )
    grad_query[...] = (joined(dot(keys.T, grad_score, ((1,), (0,)))) * SCALE).T.astype(low)
    grad_keys = dot(grad_score, query_cat, ((1,), (0,)))
    grad_values = dot(prob_low, dout_cat, ((1,), (0,)))
    for row, out in enumerate((up, middle, down)):
        for column in range(3):
            out[column, 0] = block(grad_keys, row * 3 + column).astype(out.dtype)
            out[column, 1] = block(grad_values, row * 3 + column).astype(out.dtype)


def attention(live, query, dout, grad, near, parts):
    block_len, width = query.shape
    low, wide = query.dtype, jnp.float32
    model_width = grad.shape[1]
    steps = width // LANES
    part_width = width * model_width // parts // PART_ROWS
    one = pl.BlockSpec((block_len, LANES), lambda p: (0, p))
    two = pl.BlockSpec((2, block_len, LANES), lambda p: (0, 0, p))
    four = pl.BlockSpec((2, 2, block_len, LANES), lambda p: (0, 0, 0, p))
    pairs = pl.BlockSpec((3, 2, block_len, LANES), lambda p: (0, 0, 0, p))
    shape = jax.ShapeDtypeStruct
    return pl.pallas_call(
        attention_kernel,
        grid=(steps,),
        in_specs=[pl.BlockSpec(memory_space=pltpu.SMEM), one, one]
        + [pl.BlockSpec((block_len, model_width), lambda p: (0, 0))]
        + [one, one, two, two, four, two, four, two],
        out_specs=[
            pl.BlockSpec((parts // steps, PART_ROWS, part_width), lambda p: (p, 0, 0)),
            one,
            pairs,
            pairs,
            pairs,
        ],
        out_shape=[
            shape((parts, PART_ROWS, part_width), low),
            shape((block_len, width), low),
            shape((3, 2, block_len, width), low),
            shape((3, 2, block_len, width), wide),
            shape((3, 2, block_len, width), low),
        ],
        scratch_shapes=[pltpu.VMEM((9 * block_len, 2 * block_len), wide)],
        compiler_params=pltpu.CompilerParams(
            dimension_semantics=("arbitrary",), vmem_limit_bytes=40 << 20
        ),
        cost_estimate=pl.CostEstimate(
            flops=12 * 9 * block_len * block_len * width * 2,
            bytes_accessed=8 << 20,
            transcendentals=9 * block_len * block_len * (width // HDIM),
        ),
    )(live, query, dout, grad, *near)


def shards(queries, keys, values, grad_out, w_out, pattern):
    low, wide = jnp.bfloat16, jnp.float32
    query, key, value, grad = queries[0, 0, 0], keys[0, 0, 0], values[0, 0, 0], grad_out[0, 0, 0]
    block_len, att_width = query.shape
    model_width = grad.shape[1]
    lat_count, opt_count = lax.axis_size("lat"), lax.axis_size("opt")
    at_lat, at_lon = lax.axis_index("lat"), lax.axis_index("lon")

    dout = lax.dot_general(
        grad, w_out, (((1,), (1,)), ((), ())), preferred_element_type=wide
    ).astype(low)
    flags = lax.dynamic_slice(pattern, (at_lat, at_lon, 0), (1, 1, 9)).reshape(9)
    at = jnp.arange(9)
    lat_step = (1 - 2 * (at_lat % 2)) * (1 - at // 3)
    lon_step = (1 - 2 * (at_lon % 2)) * (1 - at % 3)
    direction = (lat_step + 1) * 3 + lon_step + 1
    flags = jnp.sum(jnp.where(direction[:, None] == at[None, :], flags[None, :], 0), axis=1)
    key_rows = at_lat + lat_step
    live = ((flags > 0) & (key_rows >= 0) & (key_rows < lat_count)).astype(jnp.int32)

    own = jnp.stack((key, value))
    far, partner = far_of(own), partner_of(own)
    pair_p, pair_q = lat_mates_of(jnp.stack((partner, own)))
    far_p, far_q = lat_mates_of(far)
    parts = opt_count * lat_count
    w_parts, grad_query, to_p, middle, to_q = attention(
        live, query, dout, grad, (key, value, partner, far, pair_p, far_p, pair_q, far_q), parts
    )

    w_part = jnp.sum(lax.all_to_all(w_parts, ("opt", "lat"), 0, 0).astype(wide), axis=0)
    w_part = jnp.sum(to_all(w_part, "lon"), axis=0).astype(low)
    across = model_width // w_part.shape[1]
    grad_weight = to_all(w_part, "lat").reshape(lat_count // across, across, PART_ROWS, -1)
    grad_weight = grad_weight.swapaxes(1, 2).reshape(att_width // opt_count, model_width).astype(wide)

    from_p, from_q = exchange(to_p, "lat", next_door), exchange(to_q, "lat", other_door)
    sums = middle + from_p.astype(wide) + from_q.astype(wide)
    from_far = far_of(sums[2].astype(low))
    from_partner = partner_of(sums[0].astype(low))
    owned = (sums[1] + from_partner.astype(wide) + from_far.astype(wide)).astype(low)
    return (
        grad_query[None, None, None],
        owned[0][None, None, None],
        owned[1][None, None, None],
        grad_weight,
    )


def solution(mesh):
    blocks = P("opt", "lat", "lon", None, None)
    return jax.shard_map(
        shards,
        mesh=mesh,
        in_specs=(blocks, blocks, blocks, blocks, P(), P()),
        out_specs=(blocks, blocks, blocks, P("opt", None)),
        check_vma=False,
    )
```

```python
import jax
import jax.numpy as jnp
from jax import lax
from jax.experimental import pallas as pl
from jax.experimental.pallas import tpu as pltpu
from jax.sharding import PartitionSpec as P

HDIM = 64
SCALE = HDIM ** (-0.5)
DEAD = -1e30
LANES = 2 * HDIM
PART_ROWS = 8


def exchange(array, axis, mate):
    pairs = [(i, mate(i)) for i in range(lax.axis_size(axis))]
    return lax.ppermute(array, axis, [(i, j) for i, j in pairs if 0 <= j < lax.axis_size(axis)])


def next_door(i):
    return i ^ 1


def other_door(i):
    return i - 1 if i % 2 == 0 else i + 1


def partner_of(array):
    return exchange(array, "lon", next_door)


def far_of(array):
    count = lax.axis_size("lon")
    return exchange(array, "lon", lambda i: other_door(i) % count)


def lat_mates_of(array):
    return exchange(array, "lat", next_door), exchange(array, "lat", other_door)


def attention_kernel(
    live,
    query,
    dout,
    grad,
    key,
    value,
    partner,
    far,
    near_p,
    far_p,
    near_q,
    far_q,
    grad_query,
    to_partner,
    own_column,
    far_ends,
    far_middle,
    w_own,
    prob,
):
    wide, low = jnp.float32, jnp.bfloat16
    block_len = query.shape[0]
    first_head = lax.broadcasted_iota(jnp.int32, query.shape, 1) < HDIM

    def apart(array):
        zero = jnp.zeros_like(array)
        return jnp.concatenate(
            [jnp.where(first_head, array, zero), jnp.where(first_head, zero, array)], axis=0
        )

    def joined(array):
        return jnp.concatenate([array[:HDIM, :block_len], array[HDIM:, block_len:]], axis=0)

    def nine(own, at):
        return jnp.concatenate(
            [
                partner[1, at], near_p[at], far_p[at],
                partner[0, at], own[...], far[at],
                partner[2, at], near_q[at], far_q[at],
            ],
            axis=0,
        )

    def block(array, at):
        return array[at * block_len : (at + 1) * block_len]

    def dot(left, right, dims):
        return lax.dot_general(left, right, (dims, ((), ())), preferred_element_type=wide)

    query_cat = apart(query[...] * jnp.asarray(SCALE, low))
    dout_cat = apart(dout[...])
    keys, values = nine(key, 0), nine(value, 1)

    scores = dot(keys, query_cat, ((1,), (1,)))
    row_max = None
    for at in range(9):
        part = block(scores, at) + jnp.where(live[at] > 0, 0.0, DEAD)
        prob[at * block_len : (at + 1) * block_len, :] = part
        row_max = part if row_max is None else jnp.maximum(row_max, part)
    row_max = jnp.max(row_max, axis=0, keepdims=True)
    total = None
    for at in range(9):
        part = jnp.exp(prob[at * block_len : (at + 1) * block_len, :] - row_max)
        prob[at * block_len : (at + 1) * block_len, :] = part
        total = part if total is None else total + part
    norm = 1.0 / jnp.sum(total, axis=0, keepdims=True)
    low_parts = []
    for at in range(9):
        part = prob[at * block_len : (at + 1) * block_len, :] * norm
        prob[at * block_len : (at + 1) * block_len, :] = part
        low_parts.append(part.astype(low))
    prob_low = jnp.concatenate(low_parts, axis=0)
    attended = joined(dot(values.T, prob_low, ((1,), (0,)))).astype(low)

    w_rows = dot(attended, grad[...], ((1,), (0,)))
    half = w_rows.shape[1] // 2
    first_core = live[9] == 0
    kept = jnp.where(first_core, w_rows[:, :half], w_rows[:, half:])
    given = jnp.where(first_core, w_rows[:, half:], w_rows[:, :half]).astype(low)
    width = w_own.shape[2]
    across = half // width
    for at in range(w_own.shape[0]):
        row, column = at // across * PART_ROWS, at % across * width
        w_own[at] = kept[row : row + PART_ROWS, column : column + width]
    for at in range(half // LANES):
        to_partner[6 + at] = given[:, at * LANES : (at + 1) * LANES]

    product = dout[...].T.astype(wide) * attended.astype(wide)
    row_delta = jnp.concatenate(
        [
            jnp.sum(product[:HDIM], axis=0, keepdims=True),
            jnp.sum(product[HDIM:], axis=0, keepdims=True),
        ],
        axis=1,
    )
    grad_prob = dot(values, dout_cat, ((1,), (1,)))
    grad_score = jnp.concatenate(
        [
            (
                prob[at * block_len : (at + 1) * block_len, :] * (block(grad_prob, at) - row_delta)
            ).astype(low)
            for at in range(9)
        ],
        axis=0,
    )
    grad_query[...] = (joined(dot(keys.T, grad_score, ((1,), (0,)))) * SCALE).T.astype(low)
    grad_keys = dot(grad_score, query_cat, ((1,), (0,)))
    grad_values = dot(prob_low, dout_cat, ((1,), (0,)))
    for at, array in enumerate((grad_keys, grad_values)):
        for row in range(3):
            to_partner[row * 2 + at] = block(array, row * 3).astype(low)
            own_column[row, at] = block(array, row * 3 + 1)
        far_ends[0, at] = block(array, 2).astype(low)
        far_ends[1, at] = block(array, 8).astype(low)
        far_middle[at] = block(array, 5)


def attention(live, query, dout, grad, near, parts):
    block_len, width = query.shape
    low, wide = query.dtype, jnp.float32
    model_width = grad.shape[1]
    steps = width // LANES
    half = model_width // 2
    part_width = width * half // parts // PART_ROWS
    one = pl.BlockSpec((block_len, LANES), lambda p: (0, p))
    two = pl.BlockSpec((2, block_len, LANES), lambda p: (0, 0, p))
    four = pl.BlockSpec((2, 2, block_len, LANES), lambda p: (0, 0, 0, p))
    six = pl.BlockSpec((3, 2, block_len, LANES), lambda p: (0, 0, 0, p))
    given = 6 + half // LANES
    shape = jax.ShapeDtypeStruct
    return pl.pallas_call(
        attention_kernel,
        grid=(steps,),
        in_specs=[pl.BlockSpec(memory_space=pltpu.SMEM), one, one]
        + [pl.BlockSpec((block_len, model_width), lambda p: (0, 0))]
        + [one, one, six, two, two, two, two, two],
        out_specs=[
            one,
            pl.BlockSpec((given, block_len, LANES), lambda p: (0, 0, p)),
            six,
            four,
            two,
            pl.BlockSpec((parts // steps, PART_ROWS, part_width), lambda p: (p, 0, 0)),
        ],
        out_shape=[
            shape((block_len, width), low),
            shape((given, block_len, width), low),
            shape((3, 2, block_len, width), wide),
            shape((2, 2, block_len, width), low),
            shape((2, block_len, width), wide),
            shape((parts, PART_ROWS, part_width), wide),
        ],
        scratch_shapes=[pltpu.VMEM((9 * block_len, 2 * block_len), wide)],
        compiler_params=pltpu.CompilerParams(
            dimension_semantics=("arbitrary",), vmem_limit_bytes=40 << 20
        ),
        cost_estimate=pl.CostEstimate(
            flops=12 * 9 * block_len * block_len * width * 2,
            bytes_accessed=8 << 20,
            transcendentals=9 * block_len * block_len * (width // HDIM),
        ),
    )(live, query, dout, grad, *near)


def chip_sum_kernel(given, own_column, far_ends, w_own, send_p, send_q, own_sum, w_parts):
    wide, low = jnp.float32, jnp.bfloat16
    for at in range(2):
        send_p[0, at] = (own_column[0, at] + given[at].astype(wide)).astype(low)
        own_sum[at] = own_column[1, at] + given[2 + at].astype(wide)
        send_q[0, at] = (own_column[2, at] + given[4 + at].astype(wide)).astype(low)
        send_p[1, at] = far_ends[0, at]
        send_q[1, at] = far_ends[1, at]
    w_given = [given[at].astype(wide) for at in range(6, given.shape[0])]
    tiles = w_parts.shape[2] // LANES
    across = len(w_given) // tiles
    for at in range(w_parts.shape[0]):
        row, first = at // across * PART_ROWS, at % across * tiles
        there = [w_given[first + tile][row : row + PART_ROWS] for tile in range(tiles)]
        w_parts[at] = (w_own[at] + jnp.concatenate(there, axis=1)).astype(low)


def chip_sum(given, own_column, far_ends, w_own):
    block_len, width = given.shape[1:]
    low, wide = given.dtype, jnp.float32
    steps = width // LANES
    two = pl.BlockSpec((2, block_len, LANES), lambda p: (0, 0, p))
    four = pl.BlockSpec((2, 2, block_len, LANES), lambda p: (0, 0, 0, p))
    six = pl.BlockSpec((3, 2, block_len, LANES), lambda p: (0, 0, 0, p))
    parts = pl.BlockSpec((w_own.shape[0] // steps,) + w_own.shape[1:], lambda p: (p, 0, 0))
    shape = jax.ShapeDtypeStruct
    return pl.pallas_call(
        chip_sum_kernel,
        grid=(steps,),
        in_specs=[
            pl.BlockSpec((given.shape[0], block_len, LANES), lambda p: (0, 0, p)),
            six,
            four,
            parts,
        ],
        out_specs=[four, four, two, parts],
        out_shape=[
            shape((2, 2, block_len, width), low),
            shape((2, 2, block_len, width), low),
            shape((2, block_len, width), wide),
            shape(w_own.shape, low),
        ],
        compiler_params=pltpu.CompilerParams(
            dimension_semantics=("arbitrary",), vmem_limit_bytes=24 << 20
        ),
        cost_estimate=pl.CostEstimate(
            flops=4 * given.size, bytes_accessed=8 * given.size, transcendentals=0
        ),
    )(given, own_column, far_ends, w_own)


def sum_and_copy(array, copies, dtype):
    def kernel(terms, out):
        total = jnp.sum(terms[...].astype(jnp.float32), axis=0).astype(dtype)
        for at in range(copies):
            out[at] = total

    return pl.pallas_call(
        kernel, out_shape=jax.ShapeDtypeStruct((copies,) + array.shape[1:], dtype)
    )(array)


def assemble(pieces, rows, columns):
    height, width = pieces.shape[1:]
    across = columns // 2 // width

    def kernel(pieces, out):
        for at in range(pieces.shape[0]):
            lat, core = at // 2, at % 2
            row, column = lat // across * height, (core * across + lat % across) * width
            out[row : row + height, column : column + width] = pieces[at].astype(jnp.float32)

    return pl.pallas_call(kernel, out_shape=jax.ShapeDtypeStruct((rows, columns), jnp.float32))(
        pieces
    )


def shards(queries, keys, values, grad_out, w_out, pattern):
    low, wide = jnp.bfloat16, jnp.float32
    query, key, value, grad = queries[0, 0, 0], keys[0, 0, 0], values[0, 0, 0], grad_out[0, 0, 0]
    block_len, att_width = query.shape
    model_width = grad.shape[1]
    lat_count, lon_count = lax.axis_size("lat"), lax.axis_size("lon")
    opt_count = lax.axis_size("opt")
    at_lat, at_lon = lax.axis_index("lat"), lax.axis_index("lon")

    dout = lax.dot_general(
        grad, w_out, (((1,), (1,)), ((), ())), preferred_element_type=wide
    ).astype(low)
    flags = lax.dynamic_slice(pattern, (at_lat, at_lon, 0), (1, 1, 9)).reshape(9)
    at = jnp.arange(9)
    lat_step = (1 - 2 * (at_lat % 2)) * (1 - at // 3)
    lon_step = (1 - 2 * (at_lon % 2)) * (1 - at % 3)
    direction = (lat_step + 1) * 3 + lon_step + 1
    flags = jnp.sum(jnp.where(direction[:, None] == at[None, :], flags[None, :], 0), axis=1)
    key_rows = at_lat + lat_step
    live = (flags > 0) & (key_rows >= 0) & (key_rows < lat_count)
    live = jnp.append(live.astype(jnp.int32), at_lon % 2)

    own = jnp.stack((key, value))
    far = far_of(own)
    near_p, near_q = lat_mates_of(own)
    partner = partner_of(jnp.stack((own, near_p, near_q)))
    far_p, far_q = lat_mates_of(far)
    parts = opt_count * lat_count
    grad_query, to_partner, own_column, far_ends, far_middle, w_own = attention(
        live, query, dout, grad, (key, value, partner, far, near_p, far_p, near_q, far_q), parts
    )

    to_p, to_q, own_sum, w_parts = chip_sum(partner_of(to_partner), own_column, far_ends, w_own)
    from_p, from_q = exchange(to_p, "lat", next_door), exchange(to_q, "lat", other_door)
    owned = own_sum + from_p[0].astype(wide) + from_q[0].astype(wide)
    far_sum = (far_middle + from_p[1].astype(wide) + from_q[1].astype(wide)).astype(low)
    owned, far_sum = lax.optimization_barrier((owned, far_sum))
    owned = (owned + far_of(far_sum).astype(wide)).astype(low)

    cores = [list(range(core, lon_count, 2)) for core in range(2)]
    chips = [
        [lat * lon_count + chip + core for lat in range(lat_count) for core in range(2)]
        for chip in range(0, lon_count, 2)
    ]
    w_part = lax.all_to_all(w_parts, ("opt", "lat"), 0, 0)
    w_part = sum_and_copy(w_part, len(cores[0]), wide)
    w_part = lax.all_to_all(w_part, "lon", 0, 0, axis_index_groups=cores)
    w_part = sum_and_copy(w_part, len(chips[0]), low)
    w_part = lax.all_to_all(w_part, ("lat", "lon"), 0, 0, axis_index_groups=chips)
    grad_weight = assemble(w_part, att_width // opt_count, model_width)

    return (
        grad_query[None, None, None],
        owned[0][None, None, None],
        owned[1][None, None, None],
        grad_weight,
    )


def solution(mesh):
    blocks = P("opt", "lat", "lon", None, None)
    return jax.shard_map(
        shards,
        mesh=mesh,
        in_specs=(blocks, blocks, blocks, blocks, P(), P()),
        out_specs=(blocks, blocks, blocks, P("opt", None)),
        check_vma=False,
    )
```

```python
import jax
import jax.numpy as jnp
from jax import lax
from jax.experimental import pallas as pl
from jax.experimental.pallas import tpu as pltpu
from jax.sharding import PartitionSpec as P

HDIM = 64
SCALE = HDIM ** (-0.5)
DEAD = -1e30
LANES = 2 * HDIM
PART_ROWS = 8


def exchange(array, axis, mate):
    pairs = [(i, mate(i)) for i in range(lax.axis_size(axis))]
    return lax.ppermute(array, axis, [(i, j) for i, j in pairs if 0 <= j < lax.axis_size(axis)])


def next_door(i):
    return i ^ 1


def other_door(i):
    return i - 1 if i % 2 == 0 else i + 1


def partner_of(array):
    return exchange(array, "lon", next_door)


def far_of(array):
    count = lax.axis_size("lon")
    return exchange(array, "lon", lambda i: other_door(i) % count)


def lat_mates_of(array):
    return exchange(array, "lat", next_door), exchange(array, "lat", other_door)


def attention_kernel(
    live,
    query,
    dout,
    grad,
    key,
    value,
    partner,
    far,
    near_p,
    far_p,
    near_q,
    far_q,
    grad_query,
    to_partner,
    w_given,
    own_column,
    far_ends,
    far_middle,
    w_own,
    weights,
):
    wide, low = jnp.float32, jnp.bfloat16
    block_len = query.shape[0]
    first_head = lax.broadcasted_iota(jnp.int32, query.shape, 1) < HDIM

    def apart(array):
        zero = jnp.zeros_like(array)
        return jnp.concatenate(
            [jnp.where(first_head, array, zero), jnp.where(first_head, zero, array)], axis=0
        )

    def joined(array):
        return jnp.concatenate([array[:HDIM, :block_len], array[HDIM:, block_len:]], axis=0)

    def nine(own, at):
        return jnp.concatenate(
            [
                partner[1, at], near_p[at], far_p[at],
                partner[0, at], own[...], far[at],
                partner[2, at], near_q[at], far_q[at],
            ],
            axis=0,
        )

    def block(array, at):
        return array[at * block_len : (at + 1) * block_len]

    def dot(left, right, dims):
        return lax.dot_general(left, right, (dims, ((), ())), preferred_element_type=wide)

    query_cat = apart(query[...] * jnp.asarray(SCALE, low))
    dout_cat = apart(dout[...])
    keys, values = nine(key, 0), nine(value, 1)

    scores = dot(keys, query_cat, ((1,), (1,)))
    shift = [jnp.where(live[at] > 0, 0.0, DEAD) for at in range(9)]
    row_max = None
    for at in range(9):
        part = jnp.max(block(scores, at), axis=0, keepdims=True) + shift[at]
        row_max = part if row_max is None else jnp.maximum(row_max, part)
    total = None
    for at in range(9):
        part = jnp.exp(block(scores, at) + (shift[at] - row_max))
        weights[at * block_len : (at + 1) * block_len, :] = part
        total = part if total is None else total + part
    norm = 1.0 / jnp.sum(total, axis=0, keepdims=True)

    def prob(at):
        return weights[at * block_len : (at + 1) * block_len, :] * norm

    low_parts = [prob(at).astype(low) for at in range(9)]
    prob_low = jnp.concatenate(low_parts, axis=0)
    attended = joined(dot(values.T, prob_low, ((1,), (0,)))).astype(low)

    w_rows = dot(attended, grad[...], ((1,), (0,)))
    half = w_rows.shape[1] // 2
    first_core = live[9] == 0
    kept = jnp.where(first_core, w_rows[:, :half], w_rows[:, half:])
    given = jnp.where(first_core, w_rows[:, half:], w_rows[:, :half]).astype(low)
    width = w_own.shape[2]
    across = half // width
    for at in range(w_own.shape[0]):
        row, column = at // across * PART_ROWS, at % across * width
        w_own[at] = kept[row : row + PART_ROWS, column : column + width]
    for at in range(half // LANES):
        w_given[at] = given[:, at * LANES : (at + 1) * LANES]

    product = dout[...].T.astype(wide) * attended.astype(wide)
    row_delta = jnp.concatenate(
        [
            jnp.sum(product[:HDIM], axis=0, keepdims=True),
            jnp.sum(product[HDIM:], axis=0, keepdims=True),
        ],
        axis=1,
    )
    grad_prob = dot(values, dout_cat, ((1,), (1,)))
    grad_score = jnp.concatenate(
        [
            (prob(at) * (block(grad_prob, at) - row_delta)).astype(low) for at in range(9)
        ],
        axis=0,
    )
    grad_query[...] = (joined(dot(keys.T, grad_score, ((1,), (0,)))) * SCALE).T.astype(low)
    grad_keys = dot(grad_score, query_cat, ((1,), (0,)))
    grad_values = dot(prob_low, dout_cat, ((1,), (0,)))
    for at, array in enumerate((grad_keys, grad_values)):
        for row in range(3):
            to_partner[row * 2 + at] = block(array, row * 3).astype(low)
            own_column[row, at] = block(array, row * 3 + 1)
        far_ends[0, at] = block(array, 2).astype(low)
        far_ends[1, at] = block(array, 8).astype(low)
        far_middle[at] = block(array, 5)


def attention(live, query, dout, grad, near, parts):
    block_len, width = query.shape
    low, wide = query.dtype, jnp.float32
    model_width = grad.shape[1]
    steps = width // LANES
    half = model_width // 2
    part_width = width * half // parts // PART_ROWS
    one = pl.BlockSpec((block_len, LANES), lambda p: (0, p))
    two = pl.BlockSpec((2, block_len, LANES), lambda p: (0, 0, p))
    four = pl.BlockSpec((2, 2, block_len, LANES), lambda p: (0, 0, 0, p))
    six = pl.BlockSpec((3, 2, block_len, LANES), lambda p: (0, 0, 0, p))
    shape = jax.ShapeDtypeStruct
    return pl.pallas_call(
        attention_kernel,
        grid=(steps,),
        in_specs=[pl.BlockSpec(memory_space=pltpu.SMEM), one, one]
        + [pl.BlockSpec((block_len, model_width), lambda p: (0, 0))]
        + [one, one, six, two, two, two, two, two],
        out_specs=[
            one,
            pl.BlockSpec((6, block_len, LANES), lambda p: (0, 0, p)),
            pl.BlockSpec((half // LANES, block_len, LANES), lambda p: (0, 0, p)),
            six,
            four,
            two,
            pl.BlockSpec((parts // steps, PART_ROWS, part_width), lambda p: (p, 0, 0)),
        ],
        out_shape=[
            shape((block_len, width), low),
            shape((6, block_len, width), low),
            shape((half // LANES, block_len, width), low),
            shape((3, 2, block_len, width), wide),
            shape((2, 2, block_len, width), low),
            shape((2, block_len, width), wide),
            shape((parts, PART_ROWS, part_width), wide),
        ],
        scratch_shapes=[pltpu.VMEM((9 * block_len, 2 * block_len), wide)],
        compiler_params=pltpu.CompilerParams(
            dimension_semantics=("arbitrary",), vmem_limit_bytes=24 << 20
        ),
        cost_estimate=pl.CostEstimate(
            flops=12 * 9 * block_len * block_len * width * 2,
            bytes_accessed=8 << 20,
            transcendentals=9 * block_len * block_len * (width // HDIM),
        ),
    )(live, query, dout, grad, *near)


def chip_sum_kernel(given, own_column, far_ends, send_p, send_q, own_sum):
    wide, low = jnp.float32, jnp.bfloat16
    for at in range(2):
        send_p[0, at] = (own_column[0, at] + given[at].astype(wide)).astype(low)
        own_sum[at] = own_column[1, at] + given[2 + at].astype(wide)
        send_q[0, at] = (own_column[2, at] + given[4 + at].astype(wide)).astype(low)
        send_p[1, at] = far_ends[0, at]
        send_q[1, at] = far_ends[1, at]


def chip_sum(given, own_column, far_ends):
    block_len, width = given.shape[1:]
    low, wide = given.dtype, jnp.float32
    two = pl.BlockSpec((2, block_len, LANES), lambda p: (0, 0, p))
    four = pl.BlockSpec((2, 2, block_len, LANES), lambda p: (0, 0, 0, p))
    six = pl.BlockSpec((3, 2, block_len, LANES), lambda p: (0, 0, 0, p))
    shape = jax.ShapeDtypeStruct
    return pl.pallas_call(
        chip_sum_kernel,
        grid=(width // LANES,),
        in_specs=[pl.BlockSpec((6, block_len, LANES), lambda p: (0, 0, p)), six, four],
        out_specs=[four, four, two],
        out_shape=[
            shape((2, 2, block_len, width), low),
            shape((2, 2, block_len, width), low),
            shape((2, block_len, width), wide),
        ],
        compiler_params=pltpu.CompilerParams(
            dimension_semantics=("arbitrary",), vmem_limit_bytes=8 << 20
        ),
        cost_estimate=pl.CostEstimate(
            flops=2 * given.size, bytes_accessed=5 * given.size, transcendentals=0
        ),
    )(given, own_column, far_ends)


def lat_sum_kernel(own_sum, far_middle, from_p, from_q, owned, far_sum):
    wide = jnp.float32
    for at in range(2):
        owned[at] = own_sum[at] + from_p[0, at].astype(wide) + from_q[0, at].astype(wide)
        far = far_middle[at] + from_p[1, at].astype(wide) + from_q[1, at].astype(wide)
        far_sum[at] = far.astype(far_sum.dtype)


def lat_sum(own_sum, far_middle, from_p, from_q):
    _, block_len, width = own_sum.shape
    two = pl.BlockSpec((2, block_len, LANES), lambda p: (0, 0, p))
    four = pl.BlockSpec((2, 2, block_len, LANES), lambda p: (0, 0, 0, p))
    shape = jax.ShapeDtypeStruct
    return pl.pallas_call(
        lat_sum_kernel,
        grid=(width // LANES,),
        in_specs=[two, two, four, four],
        out_specs=[two, two],
        out_shape=[shape(own_sum.shape, own_sum.dtype), shape(own_sum.shape, from_p.dtype)],
        compiler_params=pltpu.CompilerParams(
            dimension_semantics=("arbitrary",), vmem_limit_bytes=8 << 20
        ),
        cost_estimate=pl.CostEstimate(flops=60_000_000_000, bytes_accessed=4 << 20, transcendentals=0),
    )(own_sum, far_middle, from_p, from_q)


def weight_sum_kernel(given, w_own, w_parts):
    wide, low = jnp.float32, jnp.bfloat16
    w_given = [given[at].astype(wide) for at in range(given.shape[0])]
    tiles = w_parts.shape[2] // LANES
    across = len(w_given) // tiles
    for at in range(w_parts.shape[0]):
        row, first = at // across * PART_ROWS, at % across * tiles
        there = [w_given[first + tile][row : row + PART_ROWS] for tile in range(tiles)]
        w_parts[at] = (w_own[at] + jnp.concatenate(there, axis=1)).astype(low)


def weight_sum(given, w_own):
    count, block_len, width = given.shape
    steps = width // LANES
    parts = pl.BlockSpec((w_own.shape[0] // steps,) + w_own.shape[1:], lambda p: (p, 0, 0))
    return pl.pallas_call(
        weight_sum_kernel,
        grid=(steps,),
        in_specs=[pl.BlockSpec((count, block_len, LANES), lambda p: (0, 0, p)), parts],
        out_specs=parts,
        out_shape=jax.ShapeDtypeStruct(w_own.shape, given.dtype),
        compiler_params=pltpu.CompilerParams(
            dimension_semantics=("arbitrary",), vmem_limit_bytes=8 << 20
        ),
        cost_estimate=pl.CostEstimate(
            flops=w_own.size, bytes_accessed=8 * w_own.size, transcendentals=0
        ),
    )(given, w_own)


def sum_and_copy(array, copies, dtype):
    def kernel(terms, out):
        total = jnp.sum(terms[...].astype(jnp.float32), axis=0).astype(dtype)
        for at in range(copies):
            out[at] = total

    return pl.pallas_call(
        kernel,
        in_specs=[pl.BlockSpec(memory_space=pltpu.VMEM)],
        out_specs=pl.BlockSpec(memory_space=pltpu.VMEM),
        out_shape=jax.ShapeDtypeStruct((copies,) + array.shape[1:], dtype),
        compiler_params=pltpu.CompilerParams(vmem_limit_bytes=8 << 20),
    )(array)


def assemble(pieces, rows, columns):
    height, width = pieces.shape[1:]
    across = columns // 2 // width

    def kernel(pieces, out):
        for at in range(pieces.shape[0]):
            lat, core = at // 2, at % 2
            row, column = lat // across * height, (core * across + lat % across) * width
            out[row : row + height, column : column + width] = pieces[at].astype(jnp.float32)

    return pl.pallas_call(
        kernel,
        in_specs=[pl.BlockSpec(memory_space=pltpu.VMEM)],
        out_shape=jax.ShapeDtypeStruct((rows, columns), jnp.float32),
        compiler_params=pltpu.CompilerParams(vmem_limit_bytes=8 << 20),
    )(pieces)


def shards(queries, keys, values, grad_out, w_out, pattern):
    low, wide = jnp.bfloat16, jnp.float32
    query, key, value, grad = queries[0, 0, 0], keys[0, 0, 0], values[0, 0, 0], grad_out[0, 0, 0]
    block_len, att_width = query.shape
    model_width = grad.shape[1]
    lat_count, lon_count = lax.axis_size("lat"), lax.axis_size("lon")
    opt_count = lax.axis_size("opt")
    at_lat, at_lon = lax.axis_index("lat"), lax.axis_index("lon")

    dout = lax.dot_general(
        grad, w_out, (((1,), (1,)), ((), ())), preferred_element_type=wide
    ).astype(low)
    flags = lax.dynamic_slice(pattern, (at_lat, at_lon, 0), (1, 1, 9)).reshape(9)
    at = jnp.arange(9)
    lat_step = (1 - 2 * (at_lat % 2)) * (1 - at // 3)
    lon_step = (1 - 2 * (at_lon % 2)) * (1 - at % 3)
    direction = (lat_step + 1) * 3 + lon_step + 1
    flags = jnp.sum(jnp.where(direction[:, None] == at[None, :], flags[None, :], 0), axis=1)
    key_rows = at_lat + lat_step
    live = (flags > 0) & (key_rows >= 0) & (key_rows < lat_count)
    live = jnp.append(live.astype(jnp.int32), at_lon % 2)

    own = jnp.stack((key, value))
    far = far_of(own)
    near_p, near_q = lat_mates_of(own)
    partner = partner_of(jnp.stack((own, near_p, near_q)))
    far_p, far_q = lat_mates_of(far)
    parts = opt_count * lat_count
    grad_query, to_partner, w_given, own_column, far_ends, far_middle, w_own = attention(
        live, query, dout, grad, (key, value, partner, far, near_p, far_p, near_q, far_q), parts
    )

    to_p, to_q, own_sum = chip_sum(partner_of(to_partner), own_column, far_ends)
    w_parts = weight_sum(partner_of(w_given), w_own)
    from_p, from_q = exchange(to_p, "lat", next_door), exchange(to_q, "lat", other_door)
    owned, far_sum = lat_sum(own_sum, far_middle, from_p, from_q)
    owned = (owned + far_of(far_sum).astype(wide)).astype(low)

    cores = [list(range(core, lon_count, 2)) for core in range(2)]
    chips = [
        [lat * lon_count + chip + core for lat in range(lat_count) for core in range(2)]
        for chip in range(0, lon_count, 2)
    ]
    w_part = lax.all_to_all(w_parts, ("opt", "lat"), 0, 0)
    w_part = sum_and_copy(w_part, len(cores[0]), wide)
    w_part = lax.all_to_all(w_part, "lon", 0, 0, axis_index_groups=cores)
    w_part = sum_and_copy(w_part, len(chips[0]), low)
    w_part = lax.all_to_all(w_part, ("lat", "lon"), 0, 0, axis_index_groups=chips)
    grad_weight = assemble(w_part, att_width // opt_count, model_width)

    return (
        grad_query[None, None, None],
        owned[0][None, None, None],
        owned[1][None, None, None],
        grad_weight,
    )


def solution(mesh):
    blocks = P("opt", "lat", "lon", None, None)
    return jax.shard_map(
        shards,
        mesh=mesh,
        in_specs=(blocks, blocks, blocks, blocks, P(), P()),
        out_specs=(blocks, blocks, blocks, P("opt", None)),
        check_vma=False,
    )
```

```python
import jax
import jax.numpy as jnp
from jax import lax
from jax.experimental import pallas as pl
from jax.experimental.pallas import tpu as pltpu
from jax.sharding import PartitionSpec as P

HDIM = 64
SCALE = HDIM ** (-0.5)
DEAD = -1e30
LANES = 2 * HDIM
PART_ROWS = 8


def exchange(array, axis, mate):
    pairs = [(i, mate(i)) for i in range(lax.axis_size(axis))]
    return lax.ppermute(array, axis, [(i, j) for i, j in pairs if 0 <= j < lax.axis_size(axis)])


def next_door(i):
    return i ^ 1


def other_door(i):
    return i - 1 if i % 2 == 0 else i + 1


def partner_of(array):
    return exchange(array, "lon", next_door)


def far_of(array):
    count = lax.axis_size("lon")
    return exchange(array, "lon", lambda i: other_door(i) % count)


def lat_mates_of(array):
    return exchange(array, "lat", next_door), exchange(array, "lat", other_door)


def dot(left, right, dims):
    return lax.dot_general(left, right, (dims, ((), ())), preferred_element_type=jnp.float32)


def apart(array):
    first_head = lax.broadcasted_iota(jnp.int32, array.shape, 1) < HDIM
    zero = jnp.zeros_like(array)
    return jnp.concatenate(
        [jnp.where(first_head, array, zero), jnp.where(first_head, zero, array)], axis=0
    )


def joined(array):
    half = array.shape[1] // 2
    return jnp.concatenate([array[:HDIM, :half], array[HDIM:, half:]], axis=0)


def nine(own, partner, far, near_p, far_p, near_q, far_q, at):
    return jnp.concatenate(
        [
            partner[1, at], near_p[at], far_p[at],
            partner[0, at], own[...], far[at],
            partner[2, at], near_q[at], far_q[at],
        ],
        axis=0,
    )


def block(array, at):
    size = array.shape[0] // 9
    return array[at * size : (at + 1) * size]


def forward_kernel(live, query, dout, grad, key, value, *refs):
    *near, w_given, w_own, stats, weights = refs
    wide, low = jnp.float32, jnp.bfloat16
    block_len = query.shape[0]
    query_cat = apart(query[...] * jnp.asarray(SCALE, low))
    keys, values = nine(key, *near, 0), nine(value, *near, 1)

    scores = dot(keys, query_cat, ((1,), (1,)))
    shift = [jnp.where(live[at] > 0, 0.0, DEAD) for at in range(9)]
    row_max = None
    for at in range(9):
        part = jnp.max(block(scores, at), axis=0, keepdims=True) + shift[at]
        row_max = part if row_max is None else jnp.maximum(row_max, part)
    total = None
    for at in range(9):
        part = jnp.exp(block(scores, at) + (shift[at] - row_max))
        weights[at * block_len : (at + 1) * block_len, :] = part
        total = part if total is None else total + part
    norm = 1.0 / jnp.sum(total, axis=0, keepdims=True)
    prob_low = (weights[...] * norm).astype(low)
    attended = joined(dot(values.T, prob_low, ((1,), (0,)))).astype(low)

    w_rows = dot(attended, grad[...], ((1,), (0,)))
    half = w_rows.shape[1] // 2
    first_core = live[9] == 0
    kept = jnp.where(first_core, w_rows[:, :half], w_rows[:, half:])
    given = jnp.where(first_core, w_rows[:, half:], w_rows[:, :half]).astype(low)
    width = w_own.shape[2]
    across = half // width
    for at in range(w_own.shape[0]):
        row, column = at // across * PART_ROWS, at % across * width
        w_own[at] = kept[row : row + PART_ROWS, column : column + width]
    for at in range(half // LANES):
        w_given[at] = given[:, at * LANES : (at + 1) * LANES]

    product = dout[...].T.astype(wide) * attended.astype(wide)
    row_delta = jnp.concatenate(
        [
            jnp.sum(product[:HDIM], axis=0, keepdims=True),
            jnp.sum(product[HDIM:], axis=0, keepdims=True),
        ],
        axis=1,
    )
    rows = [jnp.broadcast_to(row, stats.shape[2:]) for row in (row_max, norm, row_delta)]
    for at, row in enumerate(rows):
        stats[0, at] = row


def backward_kernel(live, query, dout, key, value, *refs):
    *near, stats, grad_query, to_partner, own_column, far_ends, far_middle = refs
    low = jnp.bfloat16
    query_cat = apart(query[...] * jnp.asarray(SCALE, low))
    dout_cat = apart(dout[...])
    keys, values = nine(key, *near, 0), nine(value, *near, 1)
    row_max, norm, row_delta = (stats[0, at, :1] for at in range(3))

    scores = dot(keys, query_cat, ((1,), (1,)))
    grad_prob = dot(values, dout_cat, ((1,), (1,)))
    prob_low, grad_score = [], []
    for at in range(9):
        shift = jnp.where(live[at] > 0, 0.0, DEAD)
        prob = jnp.exp(block(scores, at) + (shift - row_max)) * norm
        prob_low.append(prob.astype(low))
        grad_score.append((prob * (block(grad_prob, at) - row_delta)).astype(low))
    prob_low = jnp.concatenate(prob_low, axis=0)
    grad_score = jnp.concatenate(grad_score, axis=0)
    grad_query[...] = (joined(dot(keys.T, grad_score, ((1,), (0,)))) * SCALE).T.astype(low)
    grad_keys = dot(grad_score, query_cat, ((1,), (0,)))
    grad_values = dot(prob_low, dout_cat, ((1,), (0,)))
    for at, array in enumerate((grad_keys, grad_values)):
        for row in range(3):
            to_partner[row * 2 + at] = block(array, row * 3).astype(low)
            own_column[row, at] = block(array, row * 3 + 1)
        far_ends[0, at] = block(array, 2).astype(low)
        far_ends[1, at] = block(array, 8).astype(low)
        far_middle[at] = block(array, 5)


def attention(live, query, dout, grad, near, parts):
    block_len, width = query.shape
    low, wide = query.dtype, jnp.float32
    model_width = grad.shape[1]
    steps = width // LANES
    half = model_width // 2
    part_width = width * half // parts // PART_ROWS
    one = pl.BlockSpec((block_len, LANES), lambda p: (0, p))
    two = pl.BlockSpec((2, block_len, LANES), lambda p: (0, 0, p))
    four = pl.BlockSpec((2, 2, block_len, LANES), lambda p: (0, 0, 0, p))
    six = pl.BlockSpec((3, 2, block_len, LANES), lambda p: (0, 0, 0, p))
    scalars = pl.BlockSpec(memory_space=pltpu.SMEM)
    of_near = [one, one, six, two, two, two, two, two]
    stats_spec = pl.BlockSpec((1, 3, 8, 2 * block_len), lambda p: (p, 0, 0, 0))
    shape = jax.ShapeDtypeStruct
    params = pltpu.CompilerParams(
        dimension_semantics=("arbitrary",), vmem_limit_bytes=24 << 20
    )
    flops = 2 * 2 * 9 * block_len * block_len * width
    exps = 9 * block_len * block_len * (width // HDIM)
    w_given, w_own, stats = pl.pallas_call(
        forward_kernel,
        grid=(steps,),
        in_specs=[scalars, one, one]
        + [pl.BlockSpec((block_len, model_width), lambda p: (0, 0))]
        + of_near,
        out_specs=[
            pl.BlockSpec((half // LANES, block_len, LANES), lambda p: (0, 0, p)),
            pl.BlockSpec((parts // steps, PART_ROWS, part_width), lambda p: (p, 0, 0)),
            stats_spec,
        ],
        out_shape=[
            shape((half // LANES, block_len, width), low),
            shape((parts, PART_ROWS, part_width), wide),
            shape((steps, 3, 8, 2 * block_len), wide),
        ],
        scratch_shapes=[pltpu.VMEM((9 * block_len, 2 * block_len), wide)],
        compiler_params=params,
        cost_estimate=pl.CostEstimate(
            flops=5 * flops, bytes_accessed=5 << 20, transcendentals=exps
        ),
    )(live, query, dout, grad, *near)
    backward = pl.pallas_call(
        backward_kernel,
        grid=(steps,),
        in_specs=[scalars, one, one] + of_near + [stats_spec],
        out_specs=[
            one,
            pl.BlockSpec((6, block_len, LANES), lambda p: (0, 0, p)),
            six,
            four,
            two,
        ],
        out_shape=[
            shape((block_len, width), low),
            shape((6, block_len, width), low),
            shape((3, 2, block_len, width), wide),
            shape((2, 2, block_len, width), low),
            shape((2, block_len, width), wide),
        ],
        compiler_params=pltpu.CompilerParams(
            dimension_semantics=("arbitrary",), vmem_limit_bytes=60 << 20
        ),
        cost_estimate=pl.CostEstimate(
            flops=10 * flops, bytes_accessed=6 << 20, transcendentals=exps
        ),
    )(live, query, dout, *near, stats)
    return w_given, w_own, backward


def chip_sum_kernel(given, own_column, far_ends, send_p, send_q, own_sum):
    wide, low = jnp.float32, jnp.bfloat16
    for at in range(2):
        send_p[0, at] = (own_column[0, at] + given[at].astype(wide)).astype(low)
        own_sum[at] = own_column[1, at] + given[2 + at].astype(wide)
        send_q[0, at] = (own_column[2, at] + given[4 + at].astype(wide)).astype(low)
        send_p[1, at] = far_ends[0, at]
        send_q[1, at] = far_ends[1, at]


def chip_sum(given, own_column, far_ends):
    block_len, width = given.shape[1:]
    low, wide = given.dtype, jnp.float32
    two = pl.BlockSpec((2, block_len, LANES), lambda p: (0, 0, p))
    four = pl.BlockSpec((2, 2, block_len, LANES), lambda p: (0, 0, 0, p))
    six = pl.BlockSpec((3, 2, block_len, LANES), lambda p: (0, 0, 0, p))
    shape = jax.ShapeDtypeStruct
    return pl.pallas_call(
        chip_sum_kernel,
        grid=(width // LANES,),
        in_specs=[pl.BlockSpec((6, block_len, LANES), lambda p: (0, 0, p)), six, four],
        out_specs=[four, four, two],
        out_shape=[
            shape((2, 2, block_len, width), low),
            shape((2, 2, block_len, width), low),
            shape((2, block_len, width), wide),
        ],
        compiler_params=pltpu.CompilerParams(
            dimension_semantics=("arbitrary",), vmem_limit_bytes=8 << 20
        ),
        cost_estimate=pl.CostEstimate(
            flops=2 * given.size, bytes_accessed=5 * given.size, transcendentals=0
        ),
    )(given, own_column, far_ends)


def lat_sum_kernel(own_sum, far_middle, from_p, from_q, owned, far_sum):
    wide = jnp.float32
    for at in range(2):
        owned[at] = own_sum[at] + from_p[0, at].astype(wide) + from_q[0, at].astype(wide)
        far = far_middle[at] + from_p[1, at].astype(wide) + from_q[1, at].astype(wide)
        far_sum[at] = far.astype(far_sum.dtype)


def lat_sum(own_sum, far_middle, from_p, from_q):
    _, block_len, width = own_sum.shape
    two = pl.BlockSpec((2, block_len, LANES), lambda p: (0, 0, p))
    four = pl.BlockSpec((2, 2, block_len, LANES), lambda p: (0, 0, 0, p))
    shape = jax.ShapeDtypeStruct
    return pl.pallas_call(
        lat_sum_kernel,
        grid=(width // LANES,),
        in_specs=[two, two, four, four],
        out_specs=[two, two],
        out_shape=[shape(own_sum.shape, own_sum.dtype), shape(own_sum.shape, from_p.dtype)],
        compiler_params=pltpu.CompilerParams(
            dimension_semantics=("arbitrary",), vmem_limit_bytes=8 << 20
        ),
        cost_estimate=pl.CostEstimate(flops=100_000_000, bytes_accessed=4 << 20, transcendentals=0),
    )(own_sum, far_middle, from_p, from_q)


def weight_sum_kernel(given, w_own, w_parts):
    wide, low = jnp.float32, jnp.bfloat16
    w_given = [given[at].astype(wide) for at in range(given.shape[0])]
    tiles = w_parts.shape[2] // LANES
    across = len(w_given) // tiles
    for at in range(w_parts.shape[0]):
        row, first = at // across * PART_ROWS, at % across * tiles
        there = [w_given[first + tile][row : row + PART_ROWS] for tile in range(tiles)]
        w_parts[at] = (w_own[at] + jnp.concatenate(there, axis=1)).astype(low)


def weight_sum(given, w_own):
    count, block_len, width = given.shape
    steps = width // LANES
    parts = pl.BlockSpec((w_own.shape[0] // steps,) + w_own.shape[1:], lambda p: (p, 0, 0))
    return pl.pallas_call(
        weight_sum_kernel,
        grid=(steps,),
        in_specs=[pl.BlockSpec((count, block_len, LANES), lambda p: (0, 0, p)), parts],
        out_specs=parts,
        out_shape=jax.ShapeDtypeStruct(w_own.shape, given.dtype),
        compiler_params=pltpu.CompilerParams(
            dimension_semantics=("arbitrary",), vmem_limit_bytes=8 << 20
        ),
        cost_estimate=pl.CostEstimate(
            flops=w_own.size, bytes_accessed=8 * w_own.size, transcendentals=0
        ),
    )(given, w_own)


def sum_and_copy(array, copies, dtype):
    def kernel(terms, out):
        total = jnp.sum(terms[...].astype(jnp.float32), axis=0).astype(dtype)
        for at in range(copies):
            out[at] = total

    return pl.pallas_call(
        kernel,
        in_specs=[pl.BlockSpec(memory_space=pltpu.VMEM)],
        out_specs=pl.BlockSpec(memory_space=pltpu.VMEM),
        out_shape=jax.ShapeDtypeStruct((copies,) + array.shape[1:], dtype),
        compiler_params=pltpu.CompilerParams(vmem_limit_bytes=8 << 20),
    )(array)


def assemble(pieces, rows, columns):
    height, width = pieces.shape[1:]
    across = columns // 2 // width

    def kernel(pieces, out):
        for at in range(pieces.shape[0]):
            lat, core = at // 2, at % 2
            row, column = lat // across * height, (core * across + lat % across) * width
            out[row : row + height, column : column + width] = pieces[at].astype(jnp.float32)

    return pl.pallas_call(
        kernel,
        in_specs=[pl.BlockSpec(memory_space=pltpu.VMEM)],
        out_shape=jax.ShapeDtypeStruct((rows, columns), jnp.float32),
        compiler_params=pltpu.CompilerParams(vmem_limit_bytes=8 << 20),
    )(pieces)


def shards(queries, keys, values, grad_out, w_out, pattern):
    low, wide = jnp.bfloat16, jnp.float32
    query, key, value, grad = queries[0, 0, 0], keys[0, 0, 0], values[0, 0, 0], grad_out[0, 0, 0]
    block_len, att_width = query.shape
    model_width = grad.shape[1]
    lat_count, lon_count = lax.axis_size("lat"), lax.axis_size("lon")
    opt_count = lax.axis_size("opt")
    at_lat, at_lon = lax.axis_index("lat"), lax.axis_index("lon")

    dout = lax.dot_general(
        grad, w_out, (((1,), (1,)), ((), ())), preferred_element_type=wide
    ).astype(low)
    flags = lax.dynamic_slice(pattern, (at_lat, at_lon, 0), (1, 1, 9)).reshape(9)
    at = jnp.arange(9)
    lat_step = (1 - 2 * (at_lat % 2)) * (1 - at // 3)
    lon_step = (1 - 2 * (at_lon % 2)) * (1 - at % 3)
    direction = (lat_step + 1) * 3 + lon_step + 1
    flags = jnp.sum(jnp.where(direction[:, None] == at[None, :], flags[None, :], 0), axis=1)
    key_rows = at_lat + lat_step
    live = (flags > 0) & (key_rows >= 0) & (key_rows < lat_count)
    live = jnp.append(live.astype(jnp.int32), at_lon % 2)

    own = jnp.stack((key, value))
    far = far_of(own)
    near_p, near_q = lat_mates_of(own)
    partner = partner_of(jnp.stack((own, near_p, near_q)))
    far_p, far_q = lat_mates_of(far)
    parts = opt_count * lat_count
    w_given, w_own, backward = attention(
        live, query, dout, grad, (key, value, partner, far, near_p, far_p, near_q, far_q), parts
    )

    grad_query, to_partner, own_column, far_ends, far_middle = backward
    to_p, to_q, own_sum = chip_sum(partner_of(to_partner), own_column, far_ends)
    w_parts = weight_sum(partner_of(w_given), w_own)
    from_p, from_q = exchange(to_p, "lat", next_door), exchange(to_q, "lat", other_door)
    owned, far_sum = lat_sum(own_sum, far_middle, from_p, from_q)
    owned = (owned + far_of(far_sum).astype(wide)).astype(low)

    cores = [list(range(core, lon_count, 2)) for core in range(2)]
    chips = [
        [lat * lon_count + chip + core for lat in range(lat_count) for core in range(2)]
        for chip in range(0, lon_count, 2)
    ]
    w_part = lax.all_to_all(w_parts, ("opt", "lat"), 0, 0)
    w_part = sum_and_copy(w_part, len(cores[0]), wide)
    w_part = lax.all_to_all(w_part, "lon", 0, 0, axis_index_groups=cores)
    w_part = sum_and_copy(w_part, len(chips[0]), low)
    w_part = lax.all_to_all(w_part, ("lat", "lon"), 0, 0, axis_index_groups=chips)
    grad_weight = assemble(w_part, att_width // opt_count, model_width)

    return (
        grad_query[None, None, None],
        owned[0][None, None, None],
        owned[1][None, None, None],
        grad_weight,
    )


def solution(mesh):
    blocks = P("opt", "lat", "lon", None, None)
    return jax.shard_map(
        shards,
        mesh=mesh,
        in_specs=(blocks, blocks, blocks, blocks, P(), P()),
        out_specs=(blocks, blocks, blocks, P("opt", None)),
        check_vma=False,
    )
```

```python
import jax
import jax.numpy as jnp
from jax import lax
from jax.experimental import pallas as pl
from jax.experimental.pallas import tpu as pltpu
from jax.sharding import PartitionSpec as P

HDIM = 64
SCALE = HDIM ** (-0.5)
DEAD = -1e30
LANES = 2 * HDIM
PART_ROWS = 8


def exchange(array, axis, mate):
    pairs = [(i, mate(i)) for i in range(lax.axis_size(axis))]
    return lax.ppermute(array, axis, [(i, j) for i, j in pairs if 0 <= j < lax.axis_size(axis)])


def next_door(i):
    return i ^ 1


def other_door(i):
    return i - 1 if i % 2 == 0 else i + 1


def partner_of(array):
    return exchange(array, "lon", next_door)


def far_of(array):
    count = lax.axis_size("lon")
    return exchange(array, "lon", lambda i: other_door(i) % count)


def lat_mates_of(array):
    return exchange(array, "lat", next_door), exchange(array, "lat", other_door)


def dot(left, right, dims):
    return lax.dot_general(left, right, (dims, ((), ())), preferred_element_type=jnp.float32)


def apart(array):
    first_head = lax.broadcasted_iota(jnp.int32, array.shape, 1) < HDIM
    zero = jnp.zeros_like(array)
    return jnp.concatenate(
        [jnp.where(first_head, array, zero), jnp.where(first_head, zero, array)], axis=0
    )


def joined(array):
    half = array.shape[1] // 2
    return jnp.concatenate([array[:HDIM, :half], array[HDIM:, half:]], axis=0)


def nine(own, partner, far, near_p, far_p, near_q, far_q, at):
    return jnp.concatenate(
        [
            partner[1, at], near_p[at], far_p[at],
            partner[0, at], own[...], far[at],
            partner[2, at], near_q[at], far_q[at],
        ],
        axis=0,
    )


def block(array, at):
    size = array.shape[0] // 9
    return array[at * size : (at + 1) * size]


def forward_kernel(live, query, dout, grad, key, value, *refs):
    *near, w_given, w_own, stats, weights = refs
    wide, low = jnp.float32, jnp.bfloat16
    block_len = query.shape[0]
    query_cat = apart(query[...] * jnp.asarray(SCALE, low))
    keys, values = nine(key, *near, 0), nine(value, *near, 1)

    scores = dot(keys, query_cat, ((1,), (1,)))
    shift = [jnp.where(live[at] > 0, 0.0, DEAD) for at in range(9)]
    row_max = None
    for at in range(9):
        part = jnp.max(block(scores, at), axis=0, keepdims=True) + shift[at]
        row_max = part if row_max is None else jnp.maximum(row_max, part)
    total = None
    for at in range(9):
        part = jnp.exp(block(scores, at) + (shift[at] - row_max))
        weights[at * block_len : (at + 1) * block_len, :] = part
        total = part if total is None else total + part
    norm = 1.0 / jnp.sum(total, axis=0, keepdims=True)
    prob_low = (weights[...] * norm).astype(low)
    attended = joined(dot(values.T, prob_low, ((1,), (0,)))).astype(low)

    w_rows = dot(attended, grad[...], ((1,), (0,)))
    half = w_rows.shape[1] // 2
    first_core = live[9] == 0
    kept = jnp.where(first_core, w_rows[:, :half], w_rows[:, half:])
    given = jnp.where(first_core, w_rows[:, half:], w_rows[:, :half]).astype(low)
    width = w_own.shape[2]
    across = half // width
    for at in range(w_own.shape[0]):
        row, column = at // across * PART_ROWS, at % across * width
        w_own[at] = kept[row : row + PART_ROWS, column : column + width]
    for at in range(half // LANES):
        w_given[at] = given[:, at * LANES : (at + 1) * LANES]

    product = dout[...].T.astype(wide) * attended.astype(wide)
    row_delta = jnp.concatenate(
        [
            jnp.sum(product[:HDIM], axis=0, keepdims=True),
            jnp.sum(product[HDIM:], axis=0, keepdims=True),
        ],
        axis=1,
    )
    rows = [jnp.broadcast_to(row, stats.shape[2:]) for row in (row_max, norm, row_delta)]
    for at, row in enumerate(rows):
        stats[0, at] = row


def backward_kernel(live, query, dout, key, value, *refs):
    *near, stats, grad_query, to_partner, own_column, far_ends, far_middle = refs
    low = jnp.bfloat16
    query_cat = apart(query[...] * jnp.asarray(SCALE, low))
    dout_cat = apart(dout[...])
    keys, values = nine(key, *near, 0), nine(value, *near, 1)
    row_max, norm, row_delta = (stats[0, at, :1] for at in range(3))

    scores = dot(keys, query_cat, ((1,), (1,)))
    grad_prob = dot(values, dout_cat, ((1,), (1,)))
    prob_low, grad_score = [], []
    for at in range(9):
        shift = jnp.where(live[at] > 0, 0.0, DEAD)
        prob = jnp.exp(block(scores, at) + (shift - row_max)) * norm
        prob_low.append(prob.astype(low))
        grad_score.append((prob * (block(grad_prob, at) - row_delta)).astype(low))
    prob_low = jnp.concatenate(prob_low, axis=0)
    grad_score = jnp.concatenate(grad_score, axis=0)
    grad_query[...] = (joined(dot(keys.T, grad_score, ((1,), (0,)))) * SCALE).T.astype(low)
    grad_keys = dot(grad_score, query_cat, ((1,), (0,)))
    grad_values = dot(prob_low, dout_cat, ((1,), (0,)))
    for at, array in enumerate((grad_keys, grad_values)):
        for row in range(3):
            to_partner[row * 2 + at] = block(array, row * 3).astype(low)
            own_column[row, at] = block(array, row * 3 + 1)
        far_ends[0, at] = block(array, 2).astype(low)
        far_ends[1, at] = block(array, 8).astype(low)
        far_middle[at] = block(array, 5)


def attention(live, query, dout, grad, near, parts):
    block_len, width = query.shape
    low, wide = query.dtype, jnp.float32
    model_width = grad.shape[1]
    steps = width // LANES
    half = model_width // 2
    part_width = width * half // parts // PART_ROWS
    one = pl.BlockSpec((block_len, LANES), lambda p: (0, p))
    two = pl.BlockSpec((2, block_len, LANES), lambda p: (0, 0, p))
    four = pl.BlockSpec((2, 2, block_len, LANES), lambda p: (0, 0, 0, p))
    six = pl.BlockSpec((3, 2, block_len, LANES), lambda p: (0, 0, 0, p))
    scalars = pl.BlockSpec(memory_space=pltpu.SMEM)
    of_near = [one, one, six, two, two, two, two, two]
    stats_spec = pl.BlockSpec((1, 3, 8, 2 * block_len), lambda p: (p, 0, 0, 0))
    shape = jax.ShapeDtypeStruct
    params = pltpu.CompilerParams(
        dimension_semantics=("arbitrary",), vmem_limit_bytes=24 << 20
    )
    flops = 2 * 2 * 9 * block_len * block_len * width
    exps = 9 * block_len * block_len * (width // HDIM)
    w_given, w_own, stats = pl.pallas_call(
        forward_kernel,
        grid=(steps,),
        in_specs=[scalars, one, one]
        + [pl.BlockSpec((block_len, model_width), lambda p: (0, 0))]
        + of_near,
        out_specs=[
            pl.BlockSpec((half // LANES, block_len, LANES), lambda p: (0, 0, p)),
            pl.BlockSpec((parts // steps, PART_ROWS, part_width), lambda p: (p, 0, 0)),
            stats_spec,
        ],
        out_shape=[
            shape((half // LANES, block_len, width), low),
            shape((parts, PART_ROWS, part_width), wide),
            shape((steps, 3, 8, 2 * block_len), wide),
        ],
        scratch_shapes=[pltpu.VMEM((9 * block_len, 2 * block_len), wide)],
        compiler_params=params,
        cost_estimate=pl.CostEstimate(
            flops=5 * flops, bytes_accessed=5 << 20, transcendentals=exps
        ),
    )(live, query, dout, grad, *near)
    backward = pl.pallas_call(
        backward_kernel,
        grid=(steps,),
        in_specs=[scalars, one, one] + of_near + [stats_spec],
        out_specs=[
            one,
            pl.BlockSpec((6, block_len, LANES), lambda p: (0, 0, p)),
            six,
            four,
            two,
        ],
        out_shape=[
            shape((block_len, width), low),
            shape((6, block_len, width), low),
            shape((3, 2, block_len, width), wide),
            shape((2, 2, block_len, width), low),
            shape((2, block_len, width), wide),
        ],
        compiler_params=pltpu.CompilerParams(
            dimension_semantics=("arbitrary",), vmem_limit_bytes=60 << 20
        ),
        cost_estimate=pl.CostEstimate(
            flops=10 * flops, bytes_accessed=6 << 20, transcendentals=exps
        ),
    )(live, query, dout, *near, stats)
    return w_given, w_own, backward


def chip_sum_kernel(given, own_column, far_ends, send_p, send_q, own_sum):
    wide, low = jnp.float32, jnp.bfloat16
    for at in range(2):
        send_p[0, at] = (own_column[0, at] + given[at].astype(wide)).astype(low)
        own_sum[at] = own_column[1, at] + given[2 + at].astype(wide)
        send_q[0, at] = (own_column[2, at] + given[4 + at].astype(wide)).astype(low)
        send_p[1, at] = far_ends[0, at]
        send_q[1, at] = far_ends[1, at]


def chip_sum(given, own_column, far_ends):
    block_len, width = given.shape[1:]
    low, wide = given.dtype, jnp.float32
    two = pl.BlockSpec((2, block_len, LANES), lambda p: (0, 0, p))
    four = pl.BlockSpec((2, 2, block_len, LANES), lambda p: (0, 0, 0, p))
    six = pl.BlockSpec((3, 2, block_len, LANES), lambda p: (0, 0, 0, p))
    shape = jax.ShapeDtypeStruct
    return pl.pallas_call(
        chip_sum_kernel,
        grid=(width // LANES,),
        in_specs=[pl.BlockSpec((6, block_len, LANES), lambda p: (0, 0, p)), six, four],
        out_specs=[four, four, two],
        out_shape=[
            shape((2, 2, block_len, width), low),
            shape((2, 2, block_len, width), low),
            shape((2, block_len, width), wide),
        ],
        compiler_params=pltpu.CompilerParams(
            dimension_semantics=("arbitrary",), vmem_limit_bytes=8 << 20
        ),
        cost_estimate=pl.CostEstimate(
            flops=2 * given.size, bytes_accessed=5 * given.size, transcendentals=0
        ),
    )(given, own_column, far_ends)


def lat_sum_kernel(own_sum, far_middle, from_p, from_q, owned, far_sum):
    wide = jnp.float32
    for at in range(2):
        owned[at] = own_sum[at] + from_p[0, at].astype(wide) + from_q[0, at].astype(wide)
        far = far_middle[at] + from_p[1, at].astype(wide) + from_q[1, at].astype(wide)
        far_sum[at] = far.astype(far_sum.dtype)


def lat_sum(own_sum, far_middle, from_p, from_q):
    _, block_len, width = own_sum.shape
    two = pl.BlockSpec((2, block_len, LANES), lambda p: (0, 0, p))
    four = pl.BlockSpec((2, 2, block_len, LANES), lambda p: (0, 0, 0, p))
    shape = jax.ShapeDtypeStruct
    return pl.pallas_call(
        lat_sum_kernel,
        grid=(width // LANES,),
        in_specs=[two, two, four, four],
        out_specs=[two, two],
        out_shape=[shape(own_sum.shape, own_sum.dtype), shape(own_sum.shape, from_p.dtype)],
        compiler_params=pltpu.CompilerParams(
            dimension_semantics=("arbitrary",), vmem_limit_bytes=8 << 20
        ),
        cost_estimate=pl.CostEstimate(flops=100_000_000, bytes_accessed=4 << 20, transcendentals=0),
    )(own_sum, far_middle, from_p, from_q)


def weight_sum_kernel(given, w_own, w_parts):
    wide, low = jnp.float32, jnp.bfloat16
    w_given = [given[at].astype(wide) for at in range(given.shape[0])]
    tiles = w_parts.shape[2] // LANES
    across = len(w_given) // tiles
    for at in range(w_parts.shape[0]):
        row, first = at // across * PART_ROWS, at % across * tiles
        there = [w_given[first + tile][row : row + PART_ROWS] for tile in range(tiles)]
        w_parts[at] = (w_own[at] + jnp.concatenate(there, axis=1)).astype(low)


def weight_sum(given, w_own):
    count, block_len, width = given.shape
    steps = width // LANES
    parts = pl.BlockSpec((w_own.shape[0] // steps,) + w_own.shape[1:], lambda p: (p, 0, 0))
    return pl.pallas_call(
        weight_sum_kernel,
        grid=(steps,),
        in_specs=[pl.BlockSpec((count, block_len, LANES), lambda p: (0, 0, p)), parts],
        out_specs=parts,
        out_shape=jax.ShapeDtypeStruct(w_own.shape, given.dtype),
        compiler_params=pltpu.CompilerParams(
            dimension_semantics=("arbitrary",), vmem_limit_bytes=8 << 20
        ),
        cost_estimate=pl.CostEstimate(
            flops=w_own.size, bytes_accessed=8 * w_own.size, transcendentals=0
        ),
    )(given, w_own)


def sum_and_copy(array, copies, dtype):
    def kernel(terms, out):
        total = jnp.sum(terms[...].astype(jnp.float32), axis=0).astype(dtype)
        for at in range(copies):
            out[at] = total

    return pl.pallas_call(
        kernel,
        in_specs=[pl.BlockSpec(memory_space=pltpu.VMEM)],
        out_specs=pl.BlockSpec(memory_space=pltpu.VMEM),
        out_shape=jax.ShapeDtypeStruct((copies,) + array.shape[1:], dtype),
        compiler_params=pltpu.CompilerParams(vmem_limit_bytes=8 << 20),
    )(array)


def assemble(pieces, rows, columns):
    height, width = pieces.shape[1:]
    across = columns // 2 // width

    def kernel(pieces, out):
        for at in range(pieces.shape[0]):
            lat, core = at // 2, at % 2
            row, column = lat // across * height, (core * across + lat % across) * width
            out[row : row + height, column : column + width] = pieces[at].astype(jnp.float32)

    return pl.pallas_call(
        kernel,
        in_specs=[pl.BlockSpec(memory_space=pltpu.VMEM)],
        out_shape=jax.ShapeDtypeStruct((rows, columns), jnp.float32),
        compiler_params=pltpu.CompilerParams(vmem_limit_bytes=8 << 20),
    )(pieces)


def shards(queries, keys, values, grad_out, w_out, pattern):
    low, wide = jnp.bfloat16, jnp.float32
    query, key, value, grad = queries[0, 0, 0], keys[0, 0, 0], values[0, 0, 0], grad_out[0, 0, 0]
    block_len, att_width = query.shape
    model_width = grad.shape[1]
    lat_count, lon_count = lax.axis_size("lat"), lax.axis_size("lon")
    opt_count = lax.axis_size("opt")
    at_lat, at_lon = lax.axis_index("lat"), lax.axis_index("lon")

    dout = lax.dot_general(
        grad, w_out, (((1,), (1,)), ((), ())), preferred_element_type=wide
    ).astype(low)
    flags = lax.dynamic_slice(pattern, (at_lat, at_lon, 0), (1, 1, 9)).reshape(9)
    at = jnp.arange(9)
    lat_step = (1 - 2 * (at_lat % 2)) * (1 - at // 3)
    lon_step = (1 - 2 * (at_lon % 2)) * (1 - at % 3)
    direction = (lat_step + 1) * 3 + lon_step + 1
    flags = jnp.sum(jnp.where(direction[:, None] == at[None, :], flags[None, :], 0), axis=1)
    key_rows = at_lat + lat_step
    live = (flags > 0) & (key_rows >= 0) & (key_rows < lat_count)
    live = jnp.append(live.astype(jnp.int32), at_lon % 2)

    own = jnp.stack((key, value))
    far = far_of(own)
    near_p, near_q = lat_mates_of(own)
    partner = partner_of(jnp.stack((own, near_p, near_q)))
    far_p, far_q = lat_mates_of(far)
    parts = opt_count * lat_count
    w_given, w_own, backward = attention(
        live, query, dout, grad, (key, value, partner, far, near_p, far_p, near_q, far_q), parts
    )

    grad_query, to_partner, own_column, far_ends, far_middle = backward
    to_p, to_q, own_sum = chip_sum(partner_of(to_partner), own_column, far_ends)
    w_parts = weight_sum(partner_of(w_given), w_own)
    from_p, from_q = exchange(to_p, "lat", next_door), exchange(to_q, "lat", other_door)
    cores = [list(range(core, lon_count, 2)) for core in range(2)]
    chips = [
        [lat * lon_count + chip + core for lat in range(lat_count) for core in range(2)]
        for chip in range(0, lon_count, 2)
    ]
    w_part = lax.all_to_all(w_parts, ("opt", "lat"), 0, 0)
    w_part = sum_and_copy(w_part, len(cores[0]), wide)
    w_part = lax.all_to_all(w_part, "lon", 0, 0, axis_index_groups=cores)
    from_p, from_q, w_part = lax.optimization_barrier((from_p, from_q, w_part))
    owned, far_sum = lat_sum(own_sum, far_middle, from_p, from_q)
    w_part = sum_and_copy(w_part, len(chips[0]), low)
    w_part = lax.all_to_all(w_part, ("lat", "lon"), 0, 0, axis_index_groups=chips)
    grad_weight = assemble(w_part, att_width // opt_count, model_width)
    owned = (owned + far_of(far_sum).astype(wide)).astype(low)

    return (
        grad_query[None, None, None],
        owned[0][None, None, None],
        owned[1][None, None, None],
        grad_weight,
    )


def solution(mesh):
    blocks = P("opt", "lat", "lon", None, None)
    return jax.shard_map(
        shards,
        mesh=mesh,
        in_specs=(blocks, blocks, blocks, blocks, P(), P()),
        out_specs=(blocks, blocks, blocks, P("opt", None)),
        check_vma=False,
    )
```

```python
import jax
import jax.numpy as jnp
from jax import lax
from jax.experimental import pallas as pl
from jax.experimental.pallas import tpu as pltpu
from jax.sharding import PartitionSpec as P

HDIM = 64
SCALE = HDIM ** (-0.5)
DEAD = -1e30
LANES = 2 * HDIM
PART_ROWS = 16
SPREAD = 4


def exchange(array, axis, mate):
    pairs = [(i, mate(i)) for i in range(lax.axis_size(axis))]
    return lax.ppermute(array, axis, [(i, j) for i, j in pairs if 0 <= j < lax.axis_size(axis)])


def next_door(i):
    return i ^ 1


def other_door(i):
    return i - 1 if i % 2 == 0 else i + 1


def partner_of(array):
    return exchange(array, "lon", next_door)


def far_of(array):
    count = lax.axis_size("lon")
    return exchange(array, "lon", lambda i: other_door(i) % count)


def lat_mates_of(array):
    return exchange(array, "lat", next_door), exchange(array, "lat", other_door)


def dot(left, right, dims):
    return lax.dot_general(left, right, (dims, ((), ())), preferred_element_type=jnp.float32)


def apart(array):
    first_head = lax.broadcasted_iota(jnp.int32, array.shape, 1) < HDIM
    zero = jnp.zeros_like(array)
    return jnp.concatenate(
        [jnp.where(first_head, array, zero), jnp.where(first_head, zero, array)], axis=0
    )


def joined(array):
    half = array.shape[1] // 2
    return jnp.concatenate([array[:HDIM, :half], array[HDIM:, half:]], axis=0)


def nine(own, partner, far, near_p, far_p, near_q, far_q, at):
    return jnp.concatenate(
        [
            partner[1, at], near_p[at], far_p[at],
            partner[0, at], own[...], far[at],
            partner[2, at], near_q[at], far_q[at],
        ],
        axis=0,
    )


def block(array, at):
    size = array.shape[0] // 9
    return array[at * size : (at + 1) * size]


def forward_kernel(live, query, dout, grad, key, value, *refs):
    *near, w_given, w_own, stats, weights = refs
    wide, low = jnp.float32, jnp.bfloat16
    block_len = query.shape[0]
    query_cat = apart(query[...] * jnp.asarray(SCALE, low))
    keys, values = nine(key, *near, 0), nine(value, *near, 1)

    scores = dot(keys, query_cat, ((1,), (1,)))
    shift = [jnp.where(live[at] > 0, 0.0, DEAD) for at in range(9)]
    row_max = None
    for at in range(9):
        part = jnp.max(block(scores, at), axis=0, keepdims=True) + shift[at]
        row_max = part if row_max is None else jnp.maximum(row_max, part)
    total = None
    for at in range(9):
        part = jnp.exp(block(scores, at) + (shift[at] - row_max))
        weights[at * block_len : (at + 1) * block_len, :] = part
        total = part if total is None else total + part
    norm = 1.0 / jnp.sum(total, axis=0, keepdims=True)
    prob_low = (weights[...] * norm).astype(low)
    attended = joined(dot(values.T, prob_low, ((1,), (0,)))).astype(low)

    w_rows = dot(attended, grad[...], ((1,), (0,)))
    half = w_rows.shape[1] // 2
    first_core = live[9] == 0
    kept = jnp.where(first_core, w_rows[:, :half], w_rows[:, half:])
    given = jnp.where(first_core, w_rows[:, half:], w_rows[:, :half]).astype(low)
    width = w_own.shape[2]
    across = half // width
    for at in range(w_own.shape[0]):
        row, column = at // across * PART_ROWS, at % across * width
        w_own[at] = kept[row : row + PART_ROWS, column : column + width]
    for at in range(half // LANES):
        w_given[at] = given[:, at * LANES : (at + 1) * LANES]

    product = dout[...].T.astype(wide) * attended.astype(wide)
    row_delta = jnp.concatenate(
        [
            jnp.sum(product[:HDIM], axis=0, keepdims=True),
            jnp.sum(product[HDIM:], axis=0, keepdims=True),
        ],
        axis=1,
    )
    rows = [jnp.broadcast_to(row, stats.shape[2:]) for row in (row_max, norm, row_delta)]
    for at, row in enumerate(rows):
        stats[0, at] = row


def backward_kernel(live, query, dout, key, value, *refs):
    *near, stats, grad_query, to_partner, own_column, far_ends, far_middle = refs
    low = jnp.bfloat16
    query_cat = apart(query[...] * jnp.asarray(SCALE, low))
    dout_cat = apart(dout[...])
    keys, values = nine(key, *near, 0), nine(value, *near, 1)
    row_max, norm, row_delta = (stats[0, at, :1] for at in range(3))

    scores = dot(keys, query_cat, ((1,), (1,)))
    grad_prob = dot(values, dout_cat, ((1,), (1,)))
    prob_low, grad_score = [], []
    for at in range(9):
        shift = jnp.where(live[at] > 0, 0.0, DEAD)
        prob = jnp.exp(block(scores, at) + (shift - row_max)) * norm
        prob_low.append(prob.astype(low))
        grad_score.append((prob * (block(grad_prob, at) - row_delta)).astype(low))
    prob_low = jnp.concatenate(prob_low, axis=0)
    grad_score = jnp.concatenate(grad_score, axis=0)
    grad_query[...] = (joined(dot(keys.T, grad_score, ((1,), (0,)))) * SCALE).T.astype(low)
    grad_keys = dot(grad_score, query_cat, ((1,), (0,)))
    grad_values = dot(prob_low, dout_cat, ((1,), (0,)))
    for at, array in enumerate((grad_keys, grad_values)):
        for row in range(3):
            to_partner[row * 2 + at] = block(array, row * 3).astype(low)
            own_column[row, at] = block(array, row * 3 + 1)
        far_ends[0, at] = block(array, 2).astype(low)
        far_ends[1, at] = block(array, 8).astype(low)
        far_middle[at] = block(array, 5)


def attention(live, query, dout, grad, near, parts):
    block_len, width = query.shape
    low, wide = query.dtype, jnp.float32
    model_width = grad.shape[1]
    steps = width // LANES
    half = model_width // 2
    part_width = width * half // parts // PART_ROWS
    one = pl.BlockSpec((block_len, LANES), lambda p: (0, p))
    two = pl.BlockSpec((2, block_len, LANES), lambda p: (0, 0, p))
    four = pl.BlockSpec((2, 2, block_len, LANES), lambda p: (0, 0, 0, p))
    six = pl.BlockSpec((3, 2, block_len, LANES), lambda p: (0, 0, 0, p))
    scalars = pl.BlockSpec(memory_space=pltpu.SMEM)
    of_near = [one, one, six, two, two, two, two, two]
    stats_spec = pl.BlockSpec((1, 3, 8, 2 * block_len), lambda p: (p, 0, 0, 0))
    shape = jax.ShapeDtypeStruct
    params = pltpu.CompilerParams(
        dimension_semantics=("arbitrary",), vmem_limit_bytes=24 << 20
    )
    flops = 2 * 2 * 9 * block_len * block_len * width
    exps = 9 * block_len * block_len * (width // HDIM)
    w_given, w_own, stats = pl.pallas_call(
        forward_kernel,
        grid=(steps,),
        in_specs=[scalars, one, one]
        + [pl.BlockSpec((block_len, model_width), lambda p: (0, 0))]
        + of_near,
        out_specs=[
            pl.BlockSpec((half // LANES, block_len, LANES), lambda p: (0, 0, p)),
            pl.BlockSpec((parts // steps, PART_ROWS, part_width), lambda p: (p, 0, 0)),
            stats_spec,
        ],
        out_shape=[
            shape((half // LANES, block_len, width), low),
            shape((parts, PART_ROWS, part_width), wide),
            shape((steps, 3, 8, 2 * block_len), wide),
        ],
        scratch_shapes=[pltpu.VMEM((9 * block_len, 2 * block_len), wide)],
        compiler_params=params,
        cost_estimate=pl.CostEstimate(
            flops=5 * flops, bytes_accessed=5 << 20, transcendentals=exps
        ),
    )(live, query, dout, grad, *near)
    backward = pl.pallas_call(
        backward_kernel,
        grid=(steps,),
        in_specs=[scalars, one, one] + of_near + [stats_spec],
        out_specs=[
            one,
            pl.BlockSpec((6, block_len, LANES), lambda p: (0, 0, p)),
            six,
            four,
            two,
        ],
        out_shape=[
            shape((block_len, width), low),
            shape((6, block_len, width), low),
            shape((3, 2, block_len, width), wide),
            shape((2, 2, block_len, width), low),
            shape((2, block_len, width), wide),
        ],
        compiler_params=pltpu.CompilerParams(
            dimension_semantics=("arbitrary",), vmem_limit_bytes=60 << 20
        ),
        cost_estimate=pl.CostEstimate(
            flops=10 * flops, bytes_accessed=6 << 20, transcendentals=exps
        ),
    )(live, query, dout, *near, stats)
    return w_given, w_own, backward


def chip_sum_kernel(given, own_column, far_ends, send_p, send_q, own_sum):
    wide, low = jnp.float32, jnp.bfloat16
    for at in range(2):
        send_p[0, at] = (own_column[0, at] + given[at].astype(wide)).astype(low)
        own_sum[at] = own_column[1, at] + given[2 + at].astype(wide)
        send_q[0, at] = (own_column[2, at] + given[4 + at].astype(wide)).astype(low)
        send_p[1, at] = far_ends[0, at]
        send_q[1, at] = far_ends[1, at]


def chip_sum(given, own_column, far_ends):
    block_len, width = given.shape[1:]
    low, wide = given.dtype, jnp.float32
    two = pl.BlockSpec((2, block_len, LANES), lambda p: (0, 0, p))
    four = pl.BlockSpec((2, 2, block_len, LANES), lambda p: (0, 0, 0, p))
    six = pl.BlockSpec((3, 2, block_len, LANES), lambda p: (0, 0, 0, p))
    shape = jax.ShapeDtypeStruct
    return pl.pallas_call(
        chip_sum_kernel,
        grid=(width // LANES,),
        in_specs=[pl.BlockSpec((6, block_len, LANES), lambda p: (0, 0, p)), six, four],
        out_specs=[four, four, two],
        out_shape=[
            shape((2, 2, block_len, width), low),
            shape((2, 2, block_len, width), low),
            shape((2, block_len, width), wide),
        ],
        compiler_params=pltpu.CompilerParams(
            dimension_semantics=("arbitrary",), vmem_limit_bytes=8 << 20
        ),
        cost_estimate=pl.CostEstimate(
            flops=2 * given.size, bytes_accessed=5 * given.size, transcendentals=0
        ),
    )(given, own_column, far_ends)


def lat_sum_kernel(own_sum, far_middle, from_p, from_q, owned, far_sum):
    wide = jnp.float32
    for at in range(2):
        owned[at] = own_sum[at] + from_p[0, at].astype(wide) + from_q[0, at].astype(wide)
        far = far_middle[at] + from_p[1, at].astype(wide) + from_q[1, at].astype(wide)
        far_sum[at] = far.astype(far_sum.dtype)


def lat_sum(own_sum, far_middle, from_p, from_q):
    _, block_len, width = own_sum.shape
    two = pl.BlockSpec((2, block_len, LANES), lambda p: (0, 0, p))
    four = pl.BlockSpec((2, 2, block_len, LANES), lambda p: (0, 0, 0, p))
    shape = jax.ShapeDtypeStruct
    return pl.pallas_call(
        lat_sum_kernel,
        grid=(width // LANES,),
        in_specs=[two, two, four, four],
        out_specs=[two, two],
        out_shape=[shape(own_sum.shape, own_sum.dtype), shape(own_sum.shape, from_p.dtype)],
        compiler_params=pltpu.CompilerParams(
            dimension_semantics=("arbitrary",), vmem_limit_bytes=8 << 20
        ),
        cost_estimate=pl.CostEstimate(flops=1_000_000_000, bytes_accessed=4 << 20, transcendentals=0),
    )(own_sum, far_middle, from_p, from_q)


def weight_sum_kernel(given, w_own, w_parts):
    wide, low = jnp.float32, jnp.bfloat16
    w_given = [given[at].astype(wide) for at in range(given.shape[0])]
    tiles = w_parts.shape[2] // LANES
    across = len(w_given) // tiles
    for at in range(w_parts.shape[0]):
        row, first = at // across * PART_ROWS, at % across * tiles
        there = [w_given[first + tile][row : row + PART_ROWS] for tile in range(tiles)]
        w_parts[at] = (w_own[at] + jnp.concatenate(there, axis=1)).astype(low)


def weight_sum(given, w_own):
    count, block_len, width = given.shape
    steps = width // LANES
    parts = pl.BlockSpec((w_own.shape[0] // steps,) + w_own.shape[1:], lambda p: (p, 0, 0))
    return pl.pallas_call(
        weight_sum_kernel,
        grid=(steps,),
        in_specs=[pl.BlockSpec((count, block_len, LANES), lambda p: (0, 0, p)), parts],
        out_specs=parts,
        out_shape=jax.ShapeDtypeStruct(w_own.shape, given.dtype),
        compiler_params=pltpu.CompilerParams(
            dimension_semantics=("arbitrary",), vmem_limit_bytes=8 << 20
        ),
        cost_estimate=pl.CostEstimate(
            flops=w_own.size, bytes_accessed=8 * w_own.size, transcendentals=0
        ),
    )(given, w_own)


def sum_and_copy(array, copies, dtype):
    def kernel(terms, out):
        total = jnp.sum(terms[...].astype(jnp.float32), axis=0).astype(dtype)
        for at in range(copies):
            out[at] = total

    return pl.pallas_call(
        kernel,
        in_specs=[pl.BlockSpec(memory_space=pltpu.VMEM)],
        out_specs=pl.BlockSpec(memory_space=pltpu.VMEM),
        out_shape=jax.ShapeDtypeStruct((copies,) + array.shape[1:], dtype),
        compiler_params=pltpu.CompilerParams(vmem_limit_bytes=8 << 20),
    )(array)


def assemble(pieces, rows, columns):
    height, width = pieces.shape[1:]
    across = columns // 2 // width

    def kernel(pieces, out):
        for at in range(pieces.shape[0]):
            x, core = at // 2, at % 2
            row, column = x // across * height, (core * across + x % across) * width
            out[row : row + height, column : column + width] = pieces[at].astype(jnp.float32)

    return pl.pallas_call(
        kernel,
        in_specs=[pl.BlockSpec(memory_space=pltpu.VMEM)],
        out_shape=jax.ShapeDtypeStruct((rows, columns), jnp.float32),
        compiler_params=pltpu.CompilerParams(vmem_limit_bytes=8 << 20),
    )(pieces)


def shards(queries, keys, values, grad_out, w_out, pattern):
    low, wide = jnp.bfloat16, jnp.float32
    query, key, value, grad = queries[0, 0, 0], keys[0, 0, 0], values[0, 0, 0], grad_out[0, 0, 0]
    block_len, att_width = query.shape
    model_width = grad.shape[1]
    lat_count, lon_count = lax.axis_size("lat"), lax.axis_size("lon")
    opt_count = lax.axis_size("opt")
    at_lat, at_lon = lax.axis_index("lat"), lax.axis_index("lon")

    dout = lax.dot_general(
        grad, w_out, (((1,), (1,)), ((), ())), preferred_element_type=wide
    ).astype(low)
    flags = lax.dynamic_slice(pattern, (at_lat, at_lon, 0), (1, 1, 9)).reshape(9)
    at = jnp.arange(9)
    lat_step = (1 - 2 * (at_lat % 2)) * (1 - at // 3)
    lon_step = (1 - 2 * (at_lon % 2)) * (1 - at % 3)
    direction = (lat_step + 1) * 3 + lon_step + 1
    flags = jnp.sum(jnp.where(direction[:, None] == at[None, :], flags[None, :], 0), axis=1)
    key_rows = at_lat + lat_step
    live = (flags > 0) & (key_rows >= 0) & (key_rows < lat_count)
    live = jnp.append(live.astype(jnp.int32), at_lon % 2)

    own = jnp.stack((key, value))
    far = far_of(own)
    near_p, near_q = lat_mates_of(own)
    partner = partner_of(jnp.stack((own, near_p, near_q)))
    far_p, far_q = lat_mates_of(far)
    parts = opt_count * SPREAD
    w_given, w_own, backward = attention(
        live, query, dout, grad, (key, value, partner, far, near_p, far_p, near_q, far_q), parts
    )

    grad_query, to_partner, own_column, far_ends, far_middle = backward
    to_p, to_q, own_sum = chip_sum(partner_of(to_partner), own_column, far_ends)
    w_parts = weight_sum(partner_of(w_given), w_own)
    from_p, from_q = exchange(to_p, "lat", next_door), exchange(to_q, "lat", other_door)
    lines = lat_count // SPREAD
    planes = [
        [opt * lat_count + line * SPREAD + x for opt in range(opt_count) for x in range(SPREAD)]
        for line in range(lines)
    ]
    columns = [
        [
            (line * SPREAD + x) * lon_count + lon
            for line in range(lines)
            for lon in range(core, lon_count, 2)
        ]
        for x in range(SPREAD)
        for core in range(2)
    ]
    rows = [
        [(line * SPREAD + x) * lon_count + chip + core for x in range(SPREAD) for core in range(2)]
        for line in range(lines)
        for chip in range(0, lon_count, 2)
    ]
    w_part = lax.all_to_all(w_parts, ("opt", "lat"), 0, 0, axis_index_groups=planes)
    w_part, own_sum = lax.optimization_barrier((w_part, own_sum))
    w_part = sum_and_copy(w_part, len(columns[0]), low)
    w_part = lax.all_to_all(w_part, ("lat", "lon"), 0, 0, axis_index_groups=columns)
    owned, far_sum = lat_sum(own_sum, far_middle, from_p, from_q)
    w_part = sum_and_copy(w_part, len(rows[0]), low)
    w_part = lax.all_to_all(w_part, ("lat", "lon"), 0, 0, axis_index_groups=rows)
    owned = (owned + far_of(far_sum).astype(wide)).astype(low)
    w_part, owned = lax.optimization_barrier((w_part, owned))
    grad_weight = assemble(w_part, att_width // opt_count, model_width)
    return (
        grad_query[None, None, None],
        owned[0][None, None, None],
        owned[1][None, None, None],
        grad_weight,
    )


def solution(mesh):
    blocks = P("opt", "lat", "lon", None, None)
    return jax.shard_map(
        shards,
        mesh=mesh,
        in_specs=(blocks, blocks, blocks, blocks, P(), P()),
        out_specs=(blocks, blocks, blocks, P("opt", None)),
        check_vma=False,
    )
```

```python
import jax
import jax.numpy as jnp
from jax import lax
from jax.experimental import pallas as pl
from jax.experimental.pallas import tpu as pltpu
from jax.sharding import PartitionSpec as P

HDIM = 64
SCALE = HDIM ** (-0.5)
DEAD = -1e30
LANES = 2 * HDIM
PART_ROWS = 16
SPREAD = 4


def exchange(array, axis, mate):
    pairs = [(i, mate(i)) for i in range(lax.axis_size(axis))]
    return lax.ppermute(array, axis, [(i, j) for i, j in pairs if 0 <= j < lax.axis_size(axis)])


def next_door(i):
    return i ^ 1


def other_door(i):
    return i - 1 if i % 2 == 0 else i + 1


def partner_of(array):
    return exchange(array, "lon", next_door)


def far_of(array):
    count = lax.axis_size("lon")
    return exchange(array, "lon", lambda i: other_door(i) % count)


def lat_mates_of(array):
    return exchange(array, "lat", next_door), exchange(array, "lat", other_door)


def in_hbm(array):
    return pltpu.with_memory_space_constraint(array, pltpu.HBM)


def dot(left, right, dims):
    return lax.dot_general(left, right, (dims, ((), ())), preferred_element_type=jnp.float32)


def apart(array):
    first_head = lax.broadcasted_iota(jnp.int32, array.shape, 1) < HDIM
    zero = jnp.zeros_like(array)
    return jnp.concatenate(
        [jnp.where(first_head, array, zero), jnp.where(first_head, zero, array)], axis=0
    )


def joined(array):
    half = array.shape[1] // 2
    return jnp.concatenate([array[:HDIM, :half], array[HDIM:, half:]], axis=0)


def nine(own, partner, far, near_p, far_p, near_q, far_q, at):
    return jnp.concatenate(
        [
            partner[1, at], near_p[at], far_p[at],
            partner[0, at], own[...], far[at],
            partner[2, at], near_q[at], far_q[at],
        ],
        axis=0,
    )


def block(array, at):
    size = array.shape[0] // 9
    return array[at * size : (at + 1) * size]


def forward_kernel(live, query, dout, grad, key, value, *refs):
    *near, w_given, w_own, stats, weights = refs
    wide, low = jnp.float32, jnp.bfloat16
    block_len = query.shape[0]
    query_cat = apart(query[...] * jnp.asarray(SCALE, low))
    keys, values = nine(key, *near, 0), nine(value, *near, 1)

    scores = dot(keys, query_cat, ((1,), (1,)))
    shift = [jnp.where(live[at] > 0, 0.0, DEAD) for at in range(9)]
    row_max = None
    for at in range(9):
        part = jnp.max(block(scores, at), axis=0, keepdims=True) + shift[at]
        row_max = part if row_max is None else jnp.maximum(row_max, part)
    total = None
    for at in range(9):
        part = jnp.exp(block(scores, at) + (shift[at] - row_max))
        weights[at * block_len : (at + 1) * block_len, :] = part
        total = part if total is None else total + part
    norm = 1.0 / jnp.sum(total, axis=0, keepdims=True)
    prob_low = (weights[...] * norm).astype(low)
    attended = joined(dot(values.T, prob_low, ((1,), (0,)))).astype(low)

    w_rows = dot(attended, grad[...], ((1,), (0,)))
    half = w_rows.shape[1] // 2
    first_core = live[9] == 0
    kept = jnp.where(first_core, w_rows[:, :half], w_rows[:, half:])
    given = jnp.where(first_core, w_rows[:, half:], w_rows[:, :half]).astype(low)
    width = w_own.shape[2]
    across = half // width
    for at in range(w_own.shape[0]):
        row, column = at // across * PART_ROWS, at % across * width
        w_own[at] = kept[row : row + PART_ROWS, column : column + width]
    for at in range(half // LANES):
        w_given[at] = given[:, at * LANES : (at + 1) * LANES]

    product = dout[...].T.astype(wide) * attended.astype(wide)
    row_delta = jnp.concatenate(
        [
            jnp.sum(product[:HDIM], axis=0, keepdims=True),
            jnp.sum(product[HDIM:], axis=0, keepdims=True),
        ],
        axis=1,
    )
    rows = [jnp.broadcast_to(row, stats.shape[2:]) for row in (row_max, norm, row_delta)]
    for at, row in enumerate(rows):
        stats[0, at] = row


def backward_kernel(live, query, dout, key, value, *refs):
    *near, stats, grad_query, to_partner, own_column, far_ends, far_middle = refs
    low = jnp.bfloat16
    query_cat = apart(query[...] * jnp.asarray(SCALE, low))
    dout_cat = apart(dout[...])
    keys, values = nine(key, *near, 0), nine(value, *near, 1)
    row_max, norm, row_delta = (stats[0, at, :1] for at in range(3))

    scores = dot(keys, query_cat, ((1,), (1,)))
    grad_prob = dot(values, dout_cat, ((1,), (1,)))
    prob_low, grad_score = [], []
    for at in range(9):
        shift = jnp.where(live[at] > 0, 0.0, DEAD)
        prob = jnp.exp(block(scores, at) + (shift - row_max)) * norm
        prob_low.append(prob.astype(low))
        grad_score.append((prob * (block(grad_prob, at) - row_delta)).astype(low))
    prob_low = jnp.concatenate(prob_low, axis=0)
    grad_score = jnp.concatenate(grad_score, axis=0)
    grad_query[...] = (joined(dot(keys.T, grad_score, ((1,), (0,)))) * SCALE).T.astype(low)
    grad_keys = dot(grad_score, query_cat, ((1,), (0,)))
    grad_values = dot(prob_low, dout_cat, ((1,), (0,)))
    for at, array in enumerate((grad_keys, grad_values)):
        for row in range(3):
            to_partner[row * 2 + at] = block(array, row * 3).astype(low)
            own_column[row, at] = block(array, row * 3 + 1)
        far_ends[0, at] = block(array, 2).astype(low)
        far_ends[1, at] = block(array, 8).astype(low)
        far_middle[at] = block(array, 5)


def attention(live, query, dout, grad, near, parts):
    block_len, width = query.shape
    low, wide = query.dtype, jnp.float32
    model_width = grad.shape[1]
    steps = width // LANES
    half = model_width // 2
    part_width = width * half // parts // PART_ROWS
    one = pl.BlockSpec((block_len, LANES), lambda p: (0, p))
    two = pl.BlockSpec((2, block_len, LANES), lambda p: (0, 0, p))
    four = pl.BlockSpec((2, 2, block_len, LANES), lambda p: (0, 0, 0, p))
    six = pl.BlockSpec((3, 2, block_len, LANES), lambda p: (0, 0, 0, p))
    scalars = pl.BlockSpec(memory_space=pltpu.SMEM)
    of_near = [one, one, six, two, two, two, two, two]
    stats_spec = pl.BlockSpec((1, 3, 8, 2 * block_len), lambda p: (p, 0, 0, 0))
    shape = jax.ShapeDtypeStruct
    params = pltpu.CompilerParams(
        dimension_semantics=("arbitrary",), vmem_limit_bytes=24 << 20
    )
    flops = 2 * 2 * 9 * block_len * block_len * width
    exps = 9 * block_len * block_len * (width // HDIM)
    w_given, w_own, stats = pl.pallas_call(
        forward_kernel,
        grid=(steps,),
        in_specs=[scalars, one, one]
        + [pl.BlockSpec((block_len, model_width), lambda p: (0, 0))]
        + of_near,
        out_specs=[
            pl.BlockSpec((half // LANES, block_len, LANES), lambda p: (0, 0, p)),
            pl.BlockSpec((parts // steps, PART_ROWS, part_width), lambda p: (p, 0, 0)),
            stats_spec,
        ],
        out_shape=[
            shape((half // LANES, block_len, width), low),
            pltpu.HBM((parts, PART_ROWS, part_width), wide),
            pltpu.HBM((steps, 3, 8, 2 * block_len), wide),
        ],
        scratch_shapes=[pltpu.VMEM((9 * block_len, 2 * block_len), wide)],
        compiler_params=params,
        cost_estimate=pl.CostEstimate(
            flops=5 * flops, bytes_accessed=5 << 20, transcendentals=exps
        ),
    )(live, query, dout, grad, *near)
    backward = pl.pallas_call(
        backward_kernel,
        grid=(steps,),
        in_specs=[scalars, one, one] + of_near + [stats_spec],
        out_specs=[
            one,
            pl.BlockSpec((6, block_len, LANES), lambda p: (0, 0, p)),
            six,
            four,
            two,
        ],
        out_shape=[
            shape((block_len, width), low),
            shape((6, block_len, width), low),
            pltpu.HBM((3, 2, block_len, width), wide),
            pltpu.HBM((2, 2, block_len, width), low),
            pltpu.HBM((2, block_len, width), wide),
        ],
        compiler_params=pltpu.CompilerParams(
            dimension_semantics=("arbitrary",), vmem_limit_bytes=24 << 20
        ),
        cost_estimate=pl.CostEstimate(
            flops=10 * flops, bytes_accessed=6 << 20, transcendentals=exps
        ),
    )(live, query, dout, *near, in_hbm(stats))
    return w_given, w_own, backward


def chip_sum_kernel(given, own_column, far_ends, send_p, send_q, own_sum):
    wide, low = jnp.float32, jnp.bfloat16
    for at in range(2):
        send_p[0, at] = (own_column[0, at] + given[at].astype(wide)).astype(low)
        own_sum[at] = own_column[1, at] + given[2 + at].astype(wide)
        send_q[0, at] = (own_column[2, at] + given[4 + at].astype(wide)).astype(low)
        send_p[1, at] = far_ends[0, at]
        send_q[1, at] = far_ends[1, at]


def chip_sum(given, own_column, far_ends):
    block_len, width = given.shape[1:]
    low, wide = given.dtype, jnp.float32
    two = pl.BlockSpec((2, block_len, LANES), lambda p: (0, 0, p))
    four = pl.BlockSpec((2, 2, block_len, LANES), lambda p: (0, 0, 0, p))
    six = pl.BlockSpec((3, 2, block_len, LANES), lambda p: (0, 0, 0, p))
    shape = jax.ShapeDtypeStruct
    return pl.pallas_call(
        chip_sum_kernel,
        grid=(width // LANES,),
        in_specs=[pl.BlockSpec((6, block_len, LANES), lambda p: (0, 0, p)), six, four],
        out_specs=[four, four, two],
        out_shape=[
            shape((2, 2, block_len, width), low),
            shape((2, 2, block_len, width), low),
            pltpu.HBM((2, block_len, width), wide),
        ],
        compiler_params=pltpu.CompilerParams(
            dimension_semantics=("arbitrary",), vmem_limit_bytes=8 << 20
        ),
        cost_estimate=pl.CostEstimate(
            flops=2 * given.size, bytes_accessed=5 * given.size, transcendentals=0
        ),
    )(given, in_hbm(own_column), in_hbm(far_ends))


def lat_sum_kernel(own_sum, far_middle, from_p, from_q, owned, far_sum):
    wide = jnp.float32
    for at in range(2):
        owned[at] = own_sum[at] + from_p[0, at].astype(wide) + from_q[0, at].astype(wide)
        far = far_middle[at] + from_p[1, at].astype(wide) + from_q[1, at].astype(wide)
        far_sum[at] = far.astype(far_sum.dtype)


def lat_sum(own_sum, far_middle, from_p, from_q):
    _, block_len, width = own_sum.shape
    two = pl.BlockSpec((2, block_len, LANES), lambda p: (0, 0, p))
    four = pl.BlockSpec((2, 2, block_len, LANES), lambda p: (0, 0, 0, p))
    shape = jax.ShapeDtypeStruct
    return pl.pallas_call(
        lat_sum_kernel,
        grid=(width // LANES,),
        in_specs=[two, two, four, four],
        out_specs=[two, two],
        out_shape=[shape(own_sum.shape, own_sum.dtype), shape(own_sum.shape, from_p.dtype)],
        compiler_params=pltpu.CompilerParams(
            dimension_semantics=("arbitrary",), vmem_limit_bytes=8 << 20
        ),
        cost_estimate=pl.CostEstimate(flops=1_000_000_000, bytes_accessed=4 << 20, transcendentals=0),
    )(in_hbm(own_sum), in_hbm(far_middle), from_p, from_q)


def weight_sum_kernel(given, w_own, w_parts):
    wide, low = jnp.float32, jnp.bfloat16
    w_given = [given[at].astype(wide) for at in range(given.shape[0])]
    tiles = w_parts.shape[2] // LANES
    across = len(w_given) // tiles
    for at in range(w_parts.shape[0]):
        row, first = at // across * PART_ROWS, at % across * tiles
        there = [w_given[first + tile][row : row + PART_ROWS] for tile in range(tiles)]
        w_parts[at] = (w_own[at] + jnp.concatenate(there, axis=1)).astype(low)


def weight_sum(given, w_own):
    count, block_len, width = given.shape
    steps = width // LANES
    parts = pl.BlockSpec((w_own.shape[0] // steps,) + w_own.shape[1:], lambda p: (p, 0, 0))
    return pl.pallas_call(
        weight_sum_kernel,
        grid=(steps,),
        in_specs=[pl.BlockSpec((count, block_len, LANES), lambda p: (0, 0, p)), parts],
        out_specs=parts,
        out_shape=jax.ShapeDtypeStruct(w_own.shape, given.dtype),
        compiler_params=pltpu.CompilerParams(
            dimension_semantics=("arbitrary",), vmem_limit_bytes=8 << 20
        ),
        cost_estimate=pl.CostEstimate(
            flops=w_own.size, bytes_accessed=8 * w_own.size, transcendentals=0
        ),
    )(given, in_hbm(w_own))


def sum_and_copy(array, copies, dtype):
    def kernel(terms, out):
        total = jnp.sum(terms[...].astype(jnp.float32), axis=0).astype(dtype)
        for at in range(copies):
            out[at] = total

    return pl.pallas_call(
        kernel,
        in_specs=[pl.BlockSpec(memory_space=pltpu.VMEM)],
        out_specs=pl.BlockSpec(memory_space=pltpu.VMEM),
        out_shape=jax.ShapeDtypeStruct((copies,) + array.shape[1:], dtype),
        compiler_params=pltpu.CompilerParams(vmem_limit_bytes=8 << 20),
    )(array)


def assemble(pieces, rows, columns):
    height, width = pieces.shape[1:]
    across = columns // 2 // width

    def kernel(pieces, out):
        for at in range(pieces.shape[0]):
            x, core = at // 2, at % 2
            row, column = x // across * height, (core * across + x % across) * width
            out[row : row + height, column : column + width] = pieces[at].astype(jnp.float32)

    return pl.pallas_call(
        kernel,
        in_specs=[pl.BlockSpec(memory_space=pltpu.VMEM)],
        out_shape=jax.ShapeDtypeStruct((rows, columns), jnp.float32),
        compiler_params=pltpu.CompilerParams(vmem_limit_bytes=8 << 20),
    )(pieces)


def shards(queries, keys, values, grad_out, w_out, pattern):
    low, wide = jnp.bfloat16, jnp.float32
    query, key, value, grad = queries[0, 0, 0], keys[0, 0, 0], values[0, 0, 0], grad_out[0, 0, 0]
    block_len, att_width = query.shape
    model_width = grad.shape[1]
    lat_count, lon_count = lax.axis_size("lat"), lax.axis_size("lon")
    opt_count = lax.axis_size("opt")
    at_lat, at_lon = lax.axis_index("lat"), lax.axis_index("lon")

    dout = lax.dot_general(
        grad, w_out, (((1,), (1,)), ((), ())), preferred_element_type=wide
    ).astype(low)
    flags = lax.dynamic_slice(pattern, (at_lat, at_lon, 0), (1, 1, 9)).reshape(9)
    at = jnp.arange(9)
    lat_step = (1 - 2 * (at_lat % 2)) * (1 - at // 3)
    lon_step = (1 - 2 * (at_lon % 2)) * (1 - at % 3)
    direction = (lat_step + 1) * 3 + lon_step + 1
    flags = jnp.sum(jnp.where(direction[:, None] == at[None, :], flags[None, :], 0), axis=1)
    key_rows = at_lat + lat_step
    live = (flags > 0) & (key_rows >= 0) & (key_rows < lat_count)
    live = jnp.append(live.astype(jnp.int32), at_lon % 2)

    own = jnp.stack((key, value))
    far = far_of(own)
    near_p, near_q = lat_mates_of(own)
    partner = partner_of(jnp.stack((own, near_p, near_q)))
    far_p, far_q = lat_mates_of(far)
    parts = opt_count * SPREAD
    w_given, w_own, backward = attention(
        live, query, dout, grad, (key, value, partner, far, near_p, far_p, near_q, far_q), parts
    )

    grad_query, to_partner, own_column, far_ends, far_middle = backward
    to_p, to_q, own_sum = chip_sum(partner_of(to_partner), own_column, far_ends)
    w_parts = weight_sum(partner_of(w_given), w_own)
    from_p, from_q = exchange(to_p, "lat", next_door), exchange(to_q, "lat", other_door)
    lines = lat_count // SPREAD
    planes = [
        [opt * lat_count + line * SPREAD + x for opt in range(opt_count) for x in range(SPREAD)]
        for line in range(lines)
    ]
    columns = [
        [
            (line * SPREAD + x) * lon_count + lon
            for line in range(lines)
            for lon in range(core, lon_count, 2)
        ]
        for x in range(SPREAD)
        for core in range(2)
    ]
    rows = [
        [(line * SPREAD + x) * lon_count + chip + core for x in range(SPREAD) for core in range(2)]
        for line in range(lines)
        for chip in range(0, lon_count, 2)
    ]
    w_part = lax.all_to_all(w_parts, ("opt", "lat"), 0, 0, axis_index_groups=planes)
    w_part, own_sum = lax.optimization_barrier((w_part, own_sum))
    w_part = sum_and_copy(w_part, len(columns[0]), low)
    w_part = lax.all_to_all(w_part, ("lat", "lon"), 0, 0, axis_index_groups=columns)
    owned, far_sum = lat_sum(own_sum, far_middle, from_p, from_q)
    w_part = sum_and_copy(w_part, len(rows[0]), low)
    w_part = lax.all_to_all(w_part, ("lat", "lon"), 0, 0, axis_index_groups=rows)
    owned = (owned + far_of(far_sum).astype(wide)).astype(low)
    w_part, owned = lax.optimization_barrier((w_part, owned))
    grad_weight = assemble(w_part, att_width // opt_count, model_width)
    return (
        grad_query[None, None, None],
        owned[0][None, None, None],
        owned[1][None, None, None],
        grad_weight,
    )


def solution(mesh):
    blocks = P("opt", "lat", "lon", None, None)
    return jax.shard_map(
        shards,
        mesh=mesh,
        in_specs=(blocks, blocks, blocks, blocks, P(), P()),
        out_specs=(blocks, blocks, blocks, P("opt", None)),
        check_vma=False,
    )
```

```python
import jax
import jax.numpy as jnp
from jax import lax
from jax.experimental import pallas as pl
from jax.experimental.pallas import tpu as pltpu
from jax.sharding import PartitionSpec as P

HDIM = 64
SCALE = HDIM ** (-0.5)
DEAD = -1e30
LANES = 2 * HDIM
PART_ROWS = 16
SPREAD = 4


def exchange(array, axis, mate):
    pairs = [(i, mate(i)) for i in range(lax.axis_size(axis))]
    return lax.ppermute(array, axis, [(i, j) for i, j in pairs if 0 <= j < lax.axis_size(axis)])


def next_door(i):
    return i ^ 1


def other_door(i):
    return i - 1 if i % 2 == 0 else i + 1


def partner_of(array):
    return exchange(array, "lon", next_door)


def far_of(array):
    count = lax.axis_size("lon")
    return exchange(array, "lon", lambda i: other_door(i) % count)


def lat_mates_of(array):
    return exchange(array, "lat", next_door), exchange(array, "lat", other_door)


def in_hbm(array):
    return pltpu.with_memory_space_constraint(array, pltpu.HBM)


def dot(left, right, dims):
    return lax.dot_general(left, right, (dims, ((), ())), preferred_element_type=jnp.float32)


def apart(array):
    first_head = lax.broadcasted_iota(jnp.int32, array.shape, 1) < HDIM
    zero = jnp.zeros_like(array)
    return jnp.concatenate(
        [jnp.where(first_head, array, zero), jnp.where(first_head, zero, array)], axis=0
    )


def joined(array):
    half = array.shape[1] // 2
    return jnp.concatenate([array[:HDIM, :half], array[HDIM:, half:]], axis=0)


def nine(own, partner, far, near_p, far_p, near_q, far_q, at):
    return jnp.concatenate(
        [
            partner[1, at], near_p[at], far_p[at],
            partner[0, at], own[...], far[at],
            partner[2, at], near_q[at], far_q[at],
        ],
        axis=0,
    )


def block(array, at):
    size = array.shape[0] // 9
    return array[at * size : (at + 1) * size]


def forward_kernel(live, query, dout, grad, key, value, *refs):
    *near, w_given, w_own, stats, weights = refs
    wide, low = jnp.float32, jnp.bfloat16
    block_len = query.shape[0]
    query_cat = apart(query[...] * jnp.asarray(SCALE, low))
    keys, values = nine(key, *near, 0), nine(value, *near, 1)

    scores = dot(keys, query_cat, ((1,), (1,)))
    shift = [jnp.where(live[at] > 0, 0.0, DEAD) for at in range(9)]
    row_max = None
    for at in range(9):
        part = jnp.max(block(scores, at), axis=0, keepdims=True) + shift[at]
        row_max = part if row_max is None else jnp.maximum(row_max, part)
    total = None
    for at in range(9):
        part = jnp.exp(block(scores, at) + (shift[at] - row_max))
        weights[at * block_len : (at + 1) * block_len, :] = part
        total = part if total is None else total + part
    norm = 1.0 / jnp.sum(total, axis=0, keepdims=True)
    prob_low = (weights[...] * norm).astype(low)
    attended = joined(dot(values.T, prob_low, ((1,), (0,)))).astype(low)

    w_rows = dot(attended, grad[...], ((1,), (0,)))
    half = w_rows.shape[1] // 2
    first_core = live[9] == 0
    kept = jnp.where(first_core, w_rows[:, :half], w_rows[:, half:])
    given = jnp.where(first_core, w_rows[:, half:], w_rows[:, :half]).astype(low)
    width = w_own.shape[2]
    across = half // width
    for at in range(w_own.shape[0]):
        row, column = at // across * PART_ROWS, at % across * width
        w_own[at] = kept[row : row + PART_ROWS, column : column + width]
    for at in range(half // LANES):
        w_given[at] = given[:, at * LANES : (at + 1) * LANES]

    product = dout[...].T.astype(wide) * attended.astype(wide)
    row_delta = jnp.concatenate(
        [
            jnp.sum(product[:HDIM], axis=0, keepdims=True),
            jnp.sum(product[HDIM:], axis=0, keepdims=True),
        ],
        axis=1,
    )
    rows = [jnp.broadcast_to(row, stats.shape[2:]) for row in (row_max, norm, row_delta)]
    for at, row in enumerate(rows):
        stats[0, at] = row


def backward_kernel(live, query, dout, key, value, *refs):
    *near, stats, grad_query, to_partner, own_column, far_ends, far_middle = refs
    low = jnp.bfloat16
    query_cat = apart(query[...] * jnp.asarray(SCALE, low))
    dout_cat = apart(dout[...])
    keys, values = nine(key, *near, 0), nine(value, *near, 1)
    row_max, norm, row_delta = (stats[0, at, :1] for at in range(3))

    scores = dot(keys, query_cat, ((1,), (1,)))
    grad_prob = dot(values, dout_cat, ((1,), (1,)))
    prob_low, grad_score = [], []
    for at in range(9):
        shift = jnp.where(live[at] > 0, 0.0, DEAD)
        prob = jnp.exp(block(scores, at) + (shift - row_max)) * norm
        prob_low.append(prob.astype(low))
        grad_score.append((prob * (block(grad_prob, at) - row_delta)).astype(low))
    prob_low = jnp.concatenate(prob_low, axis=0)
    grad_score = jnp.concatenate(grad_score, axis=0)
    grad_query[...] = (joined(dot(keys.T, grad_score, ((1,), (0,)))) * SCALE).T.astype(low)
    grad_keys = dot(grad_score, query_cat, ((1,), (0,)))
    grad_values = dot(prob_low, dout_cat, ((1,), (0,)))
    for at, array in enumerate((grad_keys, grad_values)):
        for row in range(3):
            to_partner[row * 2 + at] = block(array, row * 3).astype(low)
            own_column[row, at] = block(array, row * 3 + 1)
        far_ends[0, at] = block(array, 2).astype(low)
        far_ends[1, at] = block(array, 8).astype(low)
        far_middle[at] = block(array, 5)


def attention(live, query, dout, grad, near, parts):
    block_len, width = query.shape
    low, wide = query.dtype, jnp.float32
    model_width = grad.shape[1]
    steps = width // LANES
    half = model_width // 2
    part_width = width * half // parts // PART_ROWS
    one = pl.BlockSpec((block_len, LANES), lambda p: (0, p))
    two = pl.BlockSpec((2, block_len, LANES), lambda p: (0, 0, p))
    four = pl.BlockSpec((2, 2, block_len, LANES), lambda p: (0, 0, 0, p))
    six = pl.BlockSpec((3, 2, block_len, LANES), lambda p: (0, 0, 0, p))
    scalars = pl.BlockSpec(memory_space=pltpu.SMEM)
    of_near = [one, one, six, two, two, two, two, two]
    stats_spec = pl.BlockSpec((1, 3, 8, 2 * block_len), lambda p: (p, 0, 0, 0))
    shape = jax.ShapeDtypeStruct
    params = pltpu.CompilerParams(
        dimension_semantics=("arbitrary",), vmem_limit_bytes=24 << 20
    )
    flops = 2 * 2 * 9 * block_len * block_len * width
    exps = 9 * block_len * block_len * (width // HDIM)
    w_given, w_own, stats = pl.pallas_call(
        forward_kernel,
        grid=(steps,),
        in_specs=[scalars, one, one]
        + [pl.BlockSpec((block_len, model_width), lambda p: (0, 0))]
        + of_near,
        out_specs=[
            pl.BlockSpec((half // LANES, block_len, LANES), lambda p: (0, 0, p)),
            pl.BlockSpec((parts // steps, PART_ROWS, part_width), lambda p: (p, 0, 0)),
            stats_spec,
        ],
        out_shape=[
            shape((half // LANES, block_len, width), low),
            pltpu.HBM((parts, PART_ROWS, part_width), wide),
            pltpu.HBM((steps, 3, 8, 2 * block_len), wide),
        ],
        scratch_shapes=[pltpu.VMEM((9 * block_len, 2 * block_len), wide)],
        compiler_params=params,
        cost_estimate=pl.CostEstimate(
            flops=5 * flops, bytes_accessed=5 << 20, transcendentals=exps
        ),
    )(live, query, dout, grad, *near)
    backward = pl.pallas_call(
        backward_kernel,
        grid=(steps,),
        in_specs=[scalars, one, one] + of_near + [stats_spec],
        out_specs=[
            one,
            pl.BlockSpec((6, block_len, LANES), lambda p: (0, 0, p)),
            six,
            four,
            two,
        ],
        out_shape=[
            shape((block_len, width), low),
            shape((6, block_len, width), low),
            pltpu.HBM((3, 2, block_len, width), wide),
            pltpu.HBM((2, 2, block_len, width), low),
            pltpu.HBM((2, block_len, width), wide),
        ],
        compiler_params=pltpu.CompilerParams(
            dimension_semantics=("arbitrary",), vmem_limit_bytes=24 << 20
        ),
        cost_estimate=pl.CostEstimate(
            flops=10 * flops, bytes_accessed=6 << 20, transcendentals=exps
        ),
    )(live, query, dout, *near, in_hbm(stats))
    return w_given, w_own, backward


def chip_sum_kernel(given, own_column, far_ends, send_p, send_q, own_sum):
    wide, low = jnp.float32, jnp.bfloat16
    for at in range(2):
        send_p[0, at] = (own_column[0, at] + given[at].astype(wide)).astype(low)
        own_sum[at] = own_column[1, at] + given[2 + at].astype(wide)
        send_q[0, at] = (own_column[2, at] + given[4 + at].astype(wide)).astype(low)
        send_p[1, at] = far_ends[0, at]
        send_q[1, at] = far_ends[1, at]


def chip_sum(given, own_column, far_ends):
    block_len, width = given.shape[1:]
    low, wide = given.dtype, jnp.float32
    rows = block_len // 2
    two = pl.BlockSpec((2, rows, width), lambda p: (0, p, 0))
    four = pl.BlockSpec((2, 2, rows, width), lambda p: (0, 0, p, 0))
    six = pl.BlockSpec((3, 2, rows, width), lambda p: (0, 0, p, 0))
    shape = jax.ShapeDtypeStruct
    return pl.pallas_call(
        chip_sum_kernel,
        grid=(2,),
        in_specs=[pl.BlockSpec((6, rows, width), lambda p: (0, p, 0)), six, four],
        out_specs=[four, four, two],
        out_shape=[
            shape((2, 2, block_len, width), low),
            shape((2, 2, block_len, width), low),
            pltpu.HBM((2, block_len, width), wide),
        ],
        compiler_params=pltpu.CompilerParams(
            dimension_semantics=("arbitrary",), vmem_limit_bytes=8 << 20
        ),
        cost_estimate=pl.CostEstimate(
            flops=2 * given.size, bytes_accessed=5 * given.size, transcendentals=0
        ),
    )(given, in_hbm(own_column), in_hbm(far_ends))


def lat_sum_kernel(own_sum, far_middle, from_p, from_q, owned, far_sum):
    wide = jnp.float32
    for at in range(2):
        owned[at] = own_sum[at] + from_p[0, at].astype(wide) + from_q[0, at].astype(wide)
        far = far_middle[at] + from_p[1, at].astype(wide) + from_q[1, at].astype(wide)
        far_sum[at] = far.astype(far_sum.dtype)


def lat_sum(own_sum, far_middle, from_p, from_q):
    _, block_len, width = own_sum.shape
    rows = block_len // 2
    two = pl.BlockSpec((2, rows, width), lambda p: (0, p, 0))
    four = pl.BlockSpec((2, 2, rows, width), lambda p: (0, 0, p, 0))
    shape = jax.ShapeDtypeStruct
    return pl.pallas_call(
        lat_sum_kernel,
        grid=(2,),
        in_specs=[two, two, four, four],
        out_specs=[two, two],
        out_shape=[shape(own_sum.shape, own_sum.dtype), shape(own_sum.shape, from_p.dtype)],
        compiler_params=pltpu.CompilerParams(
            dimension_semantics=("arbitrary",), vmem_limit_bytes=8 << 20
        ),
        cost_estimate=pl.CostEstimate(flops=1_000_000_000, bytes_accessed=4 << 20, transcendentals=0),
    )(in_hbm(own_sum), in_hbm(far_middle), from_p, from_q)


def weight_sum_kernel(given, w_own, w_parts):
    wide, low = jnp.float32, jnp.bfloat16
    count, block_len, width = given.shape
    tiles = w_parts.shape[2] // LANES
    across = count // tiles
    per_pair = w_parts.shape[0] // (width // LANES)
    for at in range(w_parts.shape[0]):
        pair, inside = at // per_pair, at % per_pair
        row, first = inside // across * PART_ROWS, inside % across * tiles
        there = [
            given[first + tile, row : row + PART_ROWS, pair * LANES : (pair + 1) * LANES]
            for tile in range(tiles)
        ]
        w_parts[at] = (w_own[at] + jnp.concatenate(there, axis=1).astype(wide)).astype(low)


def weight_sum(given, w_own):
    return pl.pallas_call(
        weight_sum_kernel,
        out_shape=jax.ShapeDtypeStruct(w_own.shape, given.dtype),
        compiler_params=pltpu.CompilerParams(vmem_limit_bytes=8 << 20),
        cost_estimate=pl.CostEstimate(
            flops=w_own.size, bytes_accessed=8 * w_own.size, transcendentals=0
        ),
    )(given, in_hbm(w_own))


def sum_and_copy(array, copies, dtype):
    def kernel(terms, out):
        total = jnp.sum(terms[...].astype(jnp.float32), axis=0).astype(dtype)
        for at in range(copies):
            out[at] = total

    return pl.pallas_call(
        kernel,
        in_specs=[pl.BlockSpec(memory_space=pltpu.VMEM)],
        out_specs=pl.BlockSpec(memory_space=pltpu.VMEM),
        out_shape=jax.ShapeDtypeStruct((copies,) + array.shape[1:], dtype),
        compiler_params=pltpu.CompilerParams(vmem_limit_bytes=8 << 20),
    )(array)


def assemble(pieces, rows, columns):
    height, width = pieces.shape[1:]
    across = columns // 2 // width

    def kernel(pieces, out):
        for at in range(pieces.shape[0]):
            x, core = at // 2, at % 2
            row, column = x // across * height, (core * across + x % across) * width
            out[row : row + height, column : column + width] = pieces[at].astype(jnp.float32)

    return pl.pallas_call(
        kernel,
        in_specs=[pl.BlockSpec(memory_space=pltpu.VMEM)],
        out_shape=jax.ShapeDtypeStruct((rows, columns), jnp.float32),
        compiler_params=pltpu.CompilerParams(vmem_limit_bytes=8 << 20),
    )(pieces)


def shards(queries, keys, values, grad_out, w_out, pattern):
    low, wide = jnp.bfloat16, jnp.float32
    query, key, value, grad = queries[0, 0, 0], keys[0, 0, 0], values[0, 0, 0], grad_out[0, 0, 0]
    block_len, att_width = query.shape
    model_width = grad.shape[1]
    lat_count, lon_count = lax.axis_size("lat"), lax.axis_size("lon")
    opt_count = lax.axis_size("opt")
    at_lat, at_lon = lax.axis_index("lat"), lax.axis_index("lon")

    dout = lax.dot_general(
        grad, w_out, (((1,), (1,)), ((), ())), preferred_element_type=wide
    ).astype(low)
    flags = lax.dynamic_slice(pattern, (at_lat, at_lon, 0), (1, 1, 9)).reshape(9)
    at = jnp.arange(9)
    lat_step = (1 - 2 * (at_lat % 2)) * (1 - at // 3)
    lon_step = (1 - 2 * (at_lon % 2)) * (1 - at % 3)
    direction = (lat_step + 1) * 3 + lon_step + 1
    flags = jnp.sum(jnp.where(direction[:, None] == at[None, :], flags[None, :], 0), axis=1)
    key_rows = at_lat + lat_step
    live = (flags > 0) & (key_rows >= 0) & (key_rows < lat_count)
    live = jnp.append(live.astype(jnp.int32), at_lon % 2)

    own = jnp.stack((key, value))
    far = far_of(own)
    near_p, near_q = lat_mates_of(own)
    partner = partner_of(jnp.stack((own, near_p, near_q)))
    far_p, far_q = lat_mates_of(far)
    parts = opt_count * SPREAD
    w_given, w_own, backward = attention(
        live, query, dout, grad, (key, value, partner, far, near_p, far_p, near_q, far_q), parts
    )

    grad_query, to_partner, own_column, far_ends, far_middle = backward
    to_p, to_q, own_sum = chip_sum(partner_of(to_partner), own_column, far_ends)
    w_parts = weight_sum(partner_of(w_given), w_own)
    from_p, from_q = exchange(to_p, "lat", next_door), exchange(to_q, "lat", other_door)
    lines = lat_count // SPREAD
    planes = [
        [opt * lat_count + line * SPREAD + x for opt in range(opt_count) for x in range(SPREAD)]
        for line in range(lines)
    ]
    columns = [
        [
            (line * SPREAD + x) * lon_count + lon
            for line in range(lines)
            for lon in range(core, lon_count, 2)
        ]
        for x in range(SPREAD)
        for core in range(2)
    ]
    rows = [
        [(line * SPREAD + x) * lon_count + chip + core for x in range(SPREAD) for core in range(2)]
        for line in range(lines)
        for chip in range(0, lon_count, 2)
    ]
    w_part = lax.all_to_all(w_parts, ("opt", "lat"), 0, 0, axis_index_groups=planes)
    w_part, own_sum = lax.optimization_barrier((w_part, own_sum))
    w_part = sum_and_copy(w_part, len(columns[0]), low)
    w_part = lax.all_to_all(w_part, ("lat", "lon"), 0, 0, axis_index_groups=columns)
    owned, far_sum = lat_sum(own_sum, far_middle, from_p, from_q)
    w_part = sum_and_copy(w_part, len(rows[0]), low)
    w_part = lax.all_to_all(w_part, ("lat", "lon"), 0, 0, axis_index_groups=rows)
    owned = (owned + far_of(far_sum).astype(wide)).astype(low)
    w_part, owned = lax.optimization_barrier((w_part, owned))
    grad_weight = assemble(w_part, att_width // opt_count, model_width)
    return (
        grad_query[None, None, None],
        owned[0][None, None, None],
        owned[1][None, None, None],
        grad_weight,
    )


def solution(mesh):
    blocks = P("opt", "lat", "lon", None, None)
    return jax.shard_map(
        shards,
        mesh=mesh,
        in_specs=(blocks, blocks, blocks, blocks, P(), P()),
        out_specs=(blocks, blocks, blocks, P("opt", None)),
        check_vma=False,
    )
```
